32 devices in a mesh: section: 2 (over x), dp: 16 (over z, y, core).
Axes of the slice: x: 2, y: 2, z: 4, core: 2. Of those that a mesh axis runs over, the one named last changes fastest.
Arguments:
- tokens: bfloat16 [4096, 768], P('dp'), may hold values from -6 to 6
- cotangent: bfloat16 [4096, 768], P('dp'), may hold values from -6 to 6
- lengths: int32 [32, 3], P('dp'), may hold values from 1 to 96, 128 in all within a row
- w_qkv: bfloat16 [2, 768, 2304], P('section', 'dp'), may hold values from -2 to 2
- w_out: bfloat16 [2, 768, 768], P('section', 'dp'), may hold values from -1.75 to 1.75
- w_in: bfloat16 [2, 768, 2304], P('section', 'dp'), may hold values from -0.21875 to 0.21875
- w_down: bfloat16 [2, 1152, 768], P('section', 'dp'), may hold values from -0.25 to 0.25
- gain_attn: bfloat16 [2, 768], P('section', 'dp'), may hold values from 0.5 to 1.5
- gain_mlp: bfloat16 [2, 768], P('section', 'dp'), may hold values from 0.5 to 1.5
Outputs:
- layer_out: bfloat16 [2, 4096, 768], P('section', 'dp')
- input_grad: bfloat16 [2, 4096, 768], P('section', 'dp')
- grad_qkv: float32 [2, 768, 2304], P('section', 'dp')
- grad_out: float32 [2, 768, 768], P('section', 'dp')
- grad_in: float32 [2, 768, 2304], P('section', 'dp')
- grad_down: float32 [2, 1152, 768], P('section', 'dp')
- grad_gain_attn: float32 [2, 768], P('section', 'dp')
- grad_gain_mlp: float32 [2, 768], P('section', 'dp')
The draws below stay inside these ranges and needn't reach their ends.
Inputs may be any that keep to these rules, and one draw needn't show every extreme that they name: Each row gives, in order, the lengths of the documents of one pack; a row sums to 128.
All inputs are finite; a program needn't handle non-finite values.
Results may differ from the reference program's by a relative error of at most 0.02.
Values may be sent and summed in bfloat16 or wider, within the bound.
A program may use at most 128 MiB of HBM per device.

```python
import math
import jax
import jax.numpy as jnp
import numpy as np
from jax import lax

D = 768
HEAD_DIM = 64
FF = 1152
WINDOW = 64
MB_TOK = 128
DOCS = 3
DOC_MOST = 96
TOKENS = 4096
PACKS = 32


def draw_w_qkv(key, part):
    first_key = jax.random.fold_in(key, 11)
    drawn = jax.random.normal(first_key, (2, D, 3 * D), jnp.float32) / math.sqrt(D)
    return jnp.clip(drawn, -2.0, 2.0).astype(jnp.bfloat16)


def block_levels(stream_key, shape, shards, least, high):
    factor_of = 1.0
    for axis_at, parts in shards:
        draws = jax.random.uniform(jax.random.fold_in(jax.random.fold_in(stream_key, 6), axis_at), (parts,), jnp.float32, least / len(shards), high / len(shards))
        factor_of = factor_of * jnp.repeat(jnp.exp(draws), shape[axis_at] // parts).reshape((-1,) + (1,) * (len(shape) - 1 - axis_at))
    return factor_of


def profile(count, total, reach, lean):
    loads = [(1 << 20) // math.isqrt(grade ** lean) + 1 for grade in range(2, count + 1)]
    rest, holding = total - reach - (count - 1), [1] * (count - 1)
    while rest > 0:
        candidates = [i for i in range(count - 1) if holding[i] < reach]
        pool, left = sum([loads[i] for i in candidates]), rest
        for i in candidates:
            extra = min(reach - holding[i], max(1, left * loads[i] // pool), rest)
            holding[i] = holding[i] + extra
            rest = rest - extra
    return np.array([reach] + holding)


def uneven_parts(rng, number_of, total, limit, slope):
    if number_of == 2:
        one = jax.random.randint(rng, (), max(1, total - limit), min(limit, total - 1) + 1)
        return jnp.stack([one, total - one])
    sizes = jnp.asarray(profile(number_of, total, limit, slope), jnp.int32)
    couples = (number_of - 1) // 2
    source_of, sink = sizes[1:1 + 2 * couples:2], sizes[2:2 + 2 * couples:2]
    room = jnp.minimum(source_of - 1, limit - sink)
    moved = jax.random.randint(jax.random.fold_in(rng, 1), (couples,), 0, 1 << 20) % (room + 1)
    sizes = sizes.at[1:1 + 2 * couples:2].set(source_of - moved).at[2:2 + 2 * couples:2].set(sink + moved)
    return sizes[jax.random.permutation(jax.random.fold_in(rng, 2), number_of)]


def normal_values(rng, extent, spread, bound, cuts=(), kind=jnp.bfloat16):
    entries = jax.random.normal(rng, extent, jnp.float32) * spread
    if len(cuts) > 0:
        entries = block_levels(rng, extent, cuts, -0.22, 0.18) * entries
    return jnp.clip(entries, min=-bound, max=bound).astype(kind)


def setup_inputs(seed: int = 0) -> dict:
    streams_of = jax.random.split(jax.random.key(seed), 10)
    tokens = normal_values(streams_of[0], (TOKENS, D), 1.0, 6.0, ((0, 16),))
    cotangent = normal_values(streams_of[1], (TOKENS, D), 1.0, 6.0, ((0, 16),))
    lengths = jax.vmap(lambda own: uneven_parts(own, DOCS, MB_TOK, DOC_MOST, 2))(jax.random.split(streams_of[2], PACKS)).reshape((PACKS, DOCS)).astype(jnp.int32)
    w_qkv = draw_w_qkv(jax.random.fold_in(streams_of[9], 71), 0)
    w_out = normal_values(streams_of[4], (2, D, D), (D // 64) ** -0.5, 1.75, ((0, 2), (1, 16)))
    w_in = normal_values(streams_of[5], (2, D, 2 * FF), D ** -0.5, 0.21875, ((0, 2), (1, 16)))
    w_down = normal_values(streams_of[6], (2, FF, D), (FF // 2) ** -0.5, 0.25, ((0, 2), (1, 16)))
    gain_attn = jnp.clip(1.0 + 0.1 * jax.random.normal(streams_of[7], (2, D), jnp.float32), 0.5, 1.5).astype(jnp.bfloat16)
    gain_mlp = jnp.clip(1.0 + 0.1 * jax.random.normal(streams_of[8], (2, D), jnp.float32), 0.5, 1.5).astype(jnp.bfloat16)
    return dict(tokens=tokens, cotangent=cotangent, lengths=lengths, w_qkv=w_qkv, w_out=w_out, w_in=w_in, w_down=w_down, gain_attn=gain_attn, gain_mlp=gain_mlp)


norm_epsilon = 1e-05

def contract(formula, left_side, right_side):
    return jnp.einsum(formula, left_side.astype(jnp.float32), right_side.astype(jnp.float32))

def layer_norm(values, gain_row):
    centered = values - lax.optimization_barrier(jnp.mean(values, axis=-1, keepdims=True))
    inverse = lax.rsqrt(lax.optimization_barrier(jnp.mean(centered * centered, axis=-1, keepdims=True)) + norm_epsilon)
    normed = centered * inverse
    return (normed * gain_row, normed, inverse)

def norm_backward(upstream, gain_row, normed, inverse):
    scaled = upstream * gain_row
    backward_part = inverse * (scaled - lax.optimization_barrier(jnp.mean(scaled, axis=-1, keepdims=True)) - normed * lax.optimization_barrier(jnp.mean(scaled * normed, axis=-1, keepdims=True)))
    return (backward_part, lax.optimization_barrier(jnp.sum(upstream * normed, axis=0)))

def pack_layout(lengths_row, row_count, window_reach):
    row_ids = jnp.arange(row_count, dtype=jnp.int32)
    doc_ends = jnp.cumsum(lengths_row).astype(jnp.int32)
    passed = row_ids[:, None] >= doc_ends[None, :]
    doc_ids = lax.optimization_barrier(jnp.sum(passed.astype(jnp.int32), axis=1)).astype(jnp.int32)
    starts = lax.optimization_barrier(jnp.max(jnp.where(passed, doc_ends[None, :], 0), axis=1)).astype(jnp.int32)
    positions = (row_ids - starts).astype(jnp.int32)
    allowed = (doc_ids[:, None] == doc_ids[None, :]) & (jnp.abs(row_ids[:, None] - row_ids[None, :]) <= window_reach)
    return (allowed, positions)

def rotation(positions, rope_base):
    half_dim = HEAD_DIM // 2
    frequency = jnp.exp(-jnp.log(rope_base) * (2.0 * jnp.arange(half_dim, dtype=jnp.float32) / HEAD_DIM))
    angles = positions.astype(jnp.float32)[:, None] * frequency[None, :]
    return (jnp.cos(angles)[:, None, :], jnp.sin(angles)[:, None, :])

def rotate(head_values, cosine, sine_part):
    half_dim = head_values.shape[-1] // 2
    first_half = head_values[..., :half_dim]
    second_half = head_values[..., half_dim:]
    return jnp.concatenate([first_half * cosine - second_half * sine_part, second_half * cosine + first_half * sine_part], axis=-1)

def score_block(queries, keys_rot, allowed):
    scores = contract('qhd,khd->hqk', queries, keys_rot) * (1.0 / jnp.sqrt(jnp.float32(HEAD_DIM)))
    return jnp.where(allowed[None], scores, -1e+30)

def layer_forward(inputs_b, weights, lengths_row, window_reach, rope_base):
    qkv_weight, out_weight, in_weight, down_weight, attn_gain, mlp_gain = weights
    row_count, model_width = inputs_b.shape
    head_count = model_width // HEAD_DIM
    residual = inputs_b.astype(jnp.float32)
    normed_in, normed_first, inverse_first = layer_norm(residual, attn_gain.astype(jnp.float32))
    ln_first = normed_in.astype(jnp.bfloat16)
    projected = jnp.dot(ln_first, qkv_weight, preferred_element_type=jnp.float32)
    allowed, positions = pack_layout(lengths_row, row_count, window_reach)
    cosine, sine_part = rotation(positions, rope_base)
    queries = rotate(projected[:, :model_width].reshape(row_count, head_count, HEAD_DIM), cosine, sine_part).astype(jnp.bfloat16)
    keys_rot = rotate(projected[:, model_width:2 * model_width].reshape(row_count, head_count, HEAD_DIM), cosine, sine_part).astype(jnp.bfloat16)
    values_b = projected[:, 2 * model_width:].astype(jnp.bfloat16).reshape(row_count, head_count, HEAD_DIM)
    scores = score_block(queries, keys_rot, allowed)
    log_total = jax.nn.logsumexp(scores, axis=-1, keepdims=True)
    attn_probs = jnp.exp(scores - log_total).astype(jnp.bfloat16)
    attended = contract('hqk,khd->qhd', attn_probs, values_b).reshape(row_count, model_width).astype(jnp.bfloat16)
    middle = residual + jnp.dot(attended, out_weight, preferred_element_type=jnp.float32)
    normed_mid, normed_second, inverse_second = layer_norm(middle, mlp_gain.astype(jnp.float32))
    ln_second = normed_mid.astype(jnp.bfloat16)
    upward = jnp.dot(ln_second, in_weight, preferred_element_type=jnp.float32)
    hidden = down_weight.shape[0]
    geglu_out = (jax.nn.gelu(upward[:, :hidden], approximate=False) * upward[:, hidden:]).astype(jnp.bfloat16)
    result = (middle + jnp.dot(geglu_out, down_weight, preferred_element_type=jnp.float32)).astype(jnp.bfloat16)
    kept_state = (ln_first, normed_first, inverse_first, queries, keys_rot, values_b, log_total, attended, normed_second, inverse_second, ln_second, upward, geglu_out, lengths_row)
    return (result, kept_state)

def layer_backward(upstream_b, kept_state, weights, window_reach, rope_base):
    qkv_weight, out_weight, in_weight, down_weight, attn_gain, mlp_gain = weights
    ln_first, normed_first, inverse_first, queries, keys_rot, values_b, log_total, attended, normed_second, inverse_second, ln_second, upward, geglu_out, lengths_row = kept_state
    row_count, model_width = upstream_b.shape
    head_count = model_width // HEAD_DIM
    hidden = down_weight.shape[0]
    upstream = upstream_b.astype(jnp.float32)
    down_grad = contract('rf,rd->fd', geglu_out, upstream_b)
    d_geglu = contract('rd,fd->rf', upstream_b, down_weight)
    gate_part = upward[:, :hidden]
    lin_part = upward[:, hidden:]
    gelu_value = jax.nn.gelu(gate_part, approximate=False)
    gelu_slope = 0.5 * (1.0 + lax.erf(gate_part / jnp.sqrt(2.0))) + gate_part * jnp.exp(-0.5 * gate_part * gate_part) / jnp.sqrt(2.0 * jnp.pi)
    d_up = jnp.concatenate([d_geglu * lin_part * gelu_slope, d_geglu * gelu_value], axis=1).astype(jnp.bfloat16)
    in_grad = contract('rd,rf->df', ln_second, d_up)
    d_ln_second = contract('rf,df->rd', d_up, in_weight)
    d_mid_norm, mlp_gain_grad = norm_backward(d_ln_second, mlp_gain.astype(jnp.float32), normed_second, inverse_second)
    d_middle = upstream + d_mid_norm
    d_middle_b = d_middle.astype(jnp.bfloat16)
    out_grad = contract('rd,re->de', attended, d_middle_b)
    d_attended = contract('re,de->rd', d_middle_b, out_weight).astype(jnp.bfloat16).reshape(row_count, head_count, HEAD_DIM)
    allowed, positions = pack_layout(lengths_row, row_count, window_reach)
    cosine, sine_part = rotation(positions, rope_base)
    scores = score_block(queries, keys_rot, allowed)
    prob_float = jnp.exp(scores - log_total)
    attn_probs = prob_float.astype(jnp.bfloat16)
    d_values = contract('hqk,qhd->khd', attn_probs, d_attended)
    d_probs = contract('qhd,khd->hqk', d_attended, values_b)
    row_delta = lax.optimization_barrier(jnp.sum(prob_float * d_probs, axis=-1, keepdims=True))
    d_scores = (prob_float * (d_probs - row_delta)).astype(jnp.bfloat16)
    score_scale = 1.0 / jnp.sqrt(jnp.float32(HEAD_DIM))
    d_queries = rotate(contract('hqk,khd->qhd', d_scores, keys_rot) * score_scale, cosine, -sine_part)
    d_keys = rotate(contract('hqk,qhd->khd', d_scores, queries) * score_scale, cosine, -sine_part)
    d_projected = jnp.concatenate([d_queries.reshape(row_count, model_width), d_keys.reshape(row_count, model_width), d_values.reshape(row_count, model_width)], axis=1).astype(jnp.bfloat16)
    qkv_grad = contract('rd,rf->df', ln_first, d_projected)
    d_ln_first = contract('rf,df->rd', d_projected, qkv_weight)
    d_in_norm, attn_gain_grad = norm_backward(d_ln_first, attn_gain.astype(jnp.float32), normed_first, inverse_first)
    d_input = (d_middle + d_in_norm).astype(jnp.bfloat16)
    return (d_input, (qkv_grad, out_grad, in_grad, down_grad, attn_gain_grad, mlp_gain_grad))

def reference(tokens, cotangent, lengths, w_qkv, w_out, w_in, w_down, gain_attn, gain_mlp):
    first_weights = (w_qkv[0], w_out[0], w_in[0], w_down[0], gain_attn[0], gain_mlp[0])
    second_weights = (w_qkv[1], w_out[1], w_in[1], w_down[1], gain_attn[1], gain_mlp[1])
    token_packs = tokens.reshape(PACKS, MB_TOK, D)
    cotangent_packs = cotangent.reshape(PACKS, MB_TOK, D)

    def step_pack(totals, packed):
        block_in, block_cot, lengths_row = packed
        middle_b, kept_first = layer_forward(block_in, first_weights, lengths_row, WINDOW, 10000.0)
        last_b, kept_second = layer_forward(middle_b, second_weights, lengths_row, MB_TOK, 160000.0)
        d_middle, grads_second = layer_backward(block_cot, kept_second, second_weights, MB_TOK, 160000.0)
        d_first, grads_first = layer_backward(d_middle, kept_first, first_weights, WINDOW, 10000.0)
        totals = jax.tree.map(lambda total_sum, first_grad, second_grad: total_sum + jnp.stack([first_grad, second_grad]), totals, grads_first, grads_second)
        return (totals, (middle_b, last_b, d_first, d_middle))
    initial = tuple((jnp.zeros((2,) + member.shape[1:], jnp.float32) for member in (w_qkv, w_out, w_in, w_down, gain_attn, gain_mlp)))
    totals, stacked = lax.scan(step_pack, initial, (token_packs, cotangent_packs, lengths))
    layer_out = jnp.stack([stacked[0].reshape(TOKENS, D), stacked[1].reshape(TOKENS, D)])
    input_grad = jnp.stack([stacked[2].reshape(TOKENS, D), stacked[3].reshape(TOKENS, D)])
    return (layer_out, input_grad, totals[0], totals[1], totals[2], totals[3], totals[4], totals[5])
```

```python
import functools

import jax
import jax.numpy as jnp
from jax import lax
from jax.experimental import pallas as pl
from jax.experimental.pallas import tpu as pltpu
from jax.sharding import PartitionSpec as P

HEAD_DIM = 64
WINDOW = 64


norm_epsilon = 1e-05


def from_behind(value, axis, steps):
    count = lax.axis_size(axis)
    leading, last = (max(0, -steps), min(count, count - steps))
    return lax.ppermute(value, axis, [(source, source + steps) for source in range(leading, last)])


def contract(formula, left_side, right_side):
    return jnp.einsum(formula, left_side, right_side, preferred_element_type=jnp.float32)


def layer_norm(values, gain_row):
    centered = values - jnp.mean(values, axis=-1, keepdims=True)
    inverse = lax.rsqrt(jnp.mean(centered * centered, axis=-1, keepdims=True) + norm_epsilon)
    normed = centered * inverse
    return (normed * gain_row, normed, inverse)


def norm_backward(upstream, gain_row, normed, inverse):
    scaled = upstream * gain_row
    backward_part = inverse * (
        scaled
        - jnp.mean(scaled, axis=-1, keepdims=True)
        - normed * jnp.mean(scaled * normed, axis=-1, keepdims=True)
    )
    return (backward_part, jnp.sum(upstream * normed, axis=0))


def pack_layout(lengths_row, row_count, window_reach):
    row_ids = jnp.arange(row_count, dtype=jnp.int32)
    doc_ends = jnp.cumsum(lengths_row)
    passed = row_ids[:, None] >= doc_ends[None, :]
    doc_ids = jnp.sum(passed.astype(jnp.int32), axis=1)
    starts = jnp.max(jnp.where(passed, doc_ends[None, :], 0), axis=1)
    positions = row_ids - starts
    allowed = (doc_ids[:, None] == doc_ids[None, :]) & (
        jnp.abs(row_ids[:, None] - row_ids[None, :]) <= window_reach
    )
    return (allowed, positions)


def rotation(positions, rope_base):
    half_dim = HEAD_DIM // 2
    frequency = jnp.exp(
        -jnp.log(rope_base) * (2.0 * jnp.arange(half_dim, dtype=jnp.float32) / HEAD_DIM)
    )
    angles = positions.astype(jnp.float32)[:, None] * frequency[None, :]
    return (jnp.cos(angles)[:, None, :], jnp.sin(angles)[:, None, :])


def rotate(head_values, cosine, sine_part):
    half_dim = head_values.shape[-1] // 2
    first_half = head_values[..., :half_dim]
    second_half = head_values[..., half_dim:]
    return jnp.concatenate(
        [
            first_half * cosine - second_half * sine_part,
            second_half * cosine + first_half * sine_part,
        ],
        axis=-1,
    )


def score_block(queries, keys_rot, allowed):
    scores = contract("qhd,khd->hqk", queries, keys_rot) * (1.0 / jnp.sqrt(jnp.float32(HEAD_DIM)))
    return jnp.where(allowed[None], scores, -1e30)


def layer_forward(inputs_b, weights, lengths_row, window_reach, rope_base):
    qkv_weight, out_weight, in_weight, down_weight, attn_gain, mlp_gain = weights
    row_count, model_width = inputs_b.shape
    head_count = model_width // HEAD_DIM
    residual = inputs_b.astype(jnp.float32)
    normed_in, normed_first, inverse_first = layer_norm(residual, attn_gain.astype(jnp.float32))
    ln_first = normed_in.astype(jnp.bfloat16)
    projected = jnp.dot(ln_first, qkv_weight, preferred_element_type=jnp.float32)
    allowed, positions = pack_layout(lengths_row, row_count, window_reach)
    cosine, sine_part = rotation(positions, rope_base)
    queries = rotate(
        projected[:, :model_width].reshape(row_count, head_count, HEAD_DIM), cosine, sine_part
    ).astype(jnp.bfloat16)
    keys_rot = rotate(
        projected[:, model_width : 2 * model_width].reshape(row_count, head_count, HEAD_DIM),
        cosine,
        sine_part,
    ).astype(jnp.bfloat16)
    values_b = (
        projected[:, 2 * model_width :]
        .astype(jnp.bfloat16)
        .reshape(row_count, head_count, HEAD_DIM)
    )
    scores = score_block(queries, keys_rot, allowed)
    log_total = jax.nn.logsumexp(scores, axis=-1, keepdims=True)
    attn_probs = jnp.exp(scores - log_total).astype(jnp.bfloat16)
    attended = (
        contract("hqk,khd->qhd", attn_probs, values_b)
        .reshape(row_count, model_width)
        .astype(jnp.bfloat16)
    )
    middle = residual + jnp.dot(attended, out_weight, preferred_element_type=jnp.float32)
    normed_mid, normed_second, inverse_second = layer_norm(middle, mlp_gain.astype(jnp.float32))
    ln_second = normed_mid.astype(jnp.bfloat16)
    upward = jnp.dot(ln_second, in_weight, preferred_element_type=jnp.float32)
    hidden = down_weight.shape[0]
    geglu_out = (jax.nn.gelu(upward[:, :hidden], approximate=False) * upward[:, hidden:]).astype(
        jnp.bfloat16
    )
    result = (middle + jnp.dot(geglu_out, down_weight, preferred_element_type=jnp.float32)).astype(
        jnp.bfloat16
    )
    kept_state = (
        ln_first,
        normed_first,
        inverse_first,
        queries,
        keys_rot,
        values_b,
        log_total,
        attended,
        normed_second,
        inverse_second,
        ln_second,
        upward,
        geglu_out,
        lengths_row,
    )
    return (result, kept_state)


def layer_backward(upstream_b, kept_state, weights, window_reach, rope_base):
    qkv_weight, out_weight, in_weight, down_weight, attn_gain, mlp_gain = weights
    (
        ln_first,
        normed_first,
        inverse_first,
        queries,
        keys_rot,
        values_b,
        log_total,
        attended,
        normed_second,
        inverse_second,
        ln_second,
        upward,
        geglu_out,
        lengths_row,
    ) = kept_state
    row_count, model_width = upstream_b.shape
    head_count = model_width // HEAD_DIM
    hidden = down_weight.shape[0]
    upstream = upstream_b.astype(jnp.float32)
    d_geglu = contract("rd,fd->rf", upstream_b, down_weight)
    gate_part = upward[:, :hidden]
    lin_part = upward[:, hidden:]
    gelu_value = jax.nn.gelu(gate_part, approximate=False)
    gelu_slope = 0.5 * (1.0 + lax.erf(gate_part / jnp.sqrt(2.0))) + gate_part * jnp.exp(
        -0.5 * gate_part * gate_part
    ) / jnp.sqrt(2.0 * jnp.pi)
    d_up = jnp.concatenate([d_geglu * lin_part * gelu_slope, d_geglu * gelu_value], axis=1).astype(
        jnp.bfloat16
    )
    d_ln_second = contract("rf,df->rd", d_up, in_weight)
    d_mid_norm, mlp_gain_grad = norm_backward(
        d_ln_second, mlp_gain.astype(jnp.float32), normed_second, inverse_second
    )
    d_middle = upstream + d_mid_norm
    d_middle_b = d_middle.astype(jnp.bfloat16)
    d_attended = (
        contract("re,de->rd", d_middle_b, out_weight)
        .astype(jnp.bfloat16)
        .reshape(row_count, head_count, HEAD_DIM)
    )
    allowed, positions = pack_layout(lengths_row, row_count, window_reach)
    cosine, sine_part = rotation(positions, rope_base)
    scores = score_block(queries, keys_rot, allowed)
    prob_float = jnp.exp(scores - log_total)
    attn_probs = prob_float.astype(jnp.bfloat16)
    d_values = contract("hqk,qhd->khd", attn_probs, d_attended)
    d_probs = contract("qhd,khd->hqk", d_attended, values_b)
    row_delta = jnp.sum(prob_float * d_probs, axis=-1, keepdims=True)
    d_scores = (prob_float * (d_probs - row_delta)).astype(jnp.bfloat16)
    score_scale = 1.0 / jnp.sqrt(jnp.float32(HEAD_DIM))
    d_queries = rotate(
        contract("hqk,khd->qhd", d_scores, keys_rot) * score_scale, cosine, -sine_part
    )
    d_keys = rotate(contract("hqk,qhd->khd", d_scores, queries) * score_scale, cosine, -sine_part)
    d_projected = jnp.concatenate(
        [
            d_queries.reshape(row_count, model_width),
            d_keys.reshape(row_count, model_width),
            d_values.reshape(row_count, model_width),
        ],
        axis=1,
    ).astype(jnp.bfloat16)
    d_ln_first = contract("rf,df->rd", d_projected, qkv_weight)
    d_in_norm, attn_gain_grad = norm_backward(
        d_ln_first, attn_gain.astype(jnp.float32), normed_first, inverse_first
    )
    d_input = (d_middle + d_in_norm).astype(jnp.bfloat16)
    return (d_input, (d_projected, d_middle_b, d_up, upstream_b, attn_gain_grad, mlp_gain_grad))


def device_at(ring_place, core, chips):
    half = ring_place // (chips // 2)
    chip = (1 - half) * 2 * ring_place + half * (2 * (chips - 1 - ring_place) + 1)
    return chip * 2 + core


def own_place(chips):
    index = lax.axis_index("dp")
    chip = index // 2
    column = chip % 2
    depth = chip // 2
    return ((1 - column) * depth + column * (chips - 1 - depth), index % 2)


def meet(right, left, sibling):
    barrier = pltpu.get_barrier_semaphore()
    for partner in (right, left, sibling):
        pl.semaphore_signal(
            barrier, inc=1, device_id={"dp": partner}, device_id_type=pl.DeviceIdType.MESH
        )
    pl.semaphore_wait(barrier, 3)


def remote(source, target, send_sem, recv_sem, partner):
    return pltpu.make_async_remote_copy(
        src_ref=source,
        dst_ref=target,
        send_sem=send_sem,
        recv_sem=recv_sem,
        device_id={"dp": partner},
        device_id_type=pl.DeviceIdType.MESH,
    )


def gather_kernel(chips, shard, full, ring_send, ring_recv, pair_send, pair_recv, own_send, own_recv, local_sem):
    place, core = own_place(chips)
    width = shard.shape[1] // 2
    right = device_at((place + 1) % chips, core, chips)
    left = device_at((place + chips - 1) % chips, core, chips)
    index = device_at(place, core, chips)
    sibling = device_at(place, 1 - core, chips)
    meet(right, left, sibling)
    keep = pltpu.make_async_copy(shard, full.at[index], local_sem)
    keep.start()
    waiting = []
    ring_copies = []
    for step in range(chips - 1):
        started = []
        for way in range(2):
            columns = pl.ds(way * width, width)
            shift = step if way == 1 else chips - step
            block = device_at((place + shift) % chips, core, chips)
            source = shard.at[:, columns] if step == 0 else full.at[block, :, columns]
            if step > 0:
                ring_copies[step - 1][way].wait_recv()
            copy = remote(
                source,
                full.at[block, :, columns],
                ring_send.at[way, step],
                ring_recv.at[way, step],
                left if way == 1 else right,
            )
            copy.start()
            started.append(copy)
            if step > 0:
                pair = remote(
                    source,
                    full.at[block, :, columns],
                    pair_send.at[way, step - 1],
                    pair_recv.at[way, step - 1],
                    sibling,
                )
                pair.start()
                waiting.append(pair)
        if step == 0:
            pair = remote(shard, full.at[index], own_send, own_recv, sibling)
            pair.start()
            waiting.append(pair)
        ring_copies.append(started)
    for way in range(2):
        ring_copies[-1][way].wait_recv()
        columns = pl.ds(way * width, width)
        shift = chips - 1 if way == 1 else 1
        block = device_at((place + shift) % chips, core, chips)
        pair = remote(
            full.at[block, :, columns],
            full.at[block, :, columns],
            pair_send.at[way, chips - 2],
            pair_recv.at[way, chips - 2],
            sibling,
        )
        pair.start()
        waiting.append(pair)
    for started in ring_copies:
        for copy in started:
            copy.wait_send()
    for pair in waiting:
        pair.wait()
    keep.wait()


def gather_all(shard):
    count = lax.axis_size("dp")
    chips = count // 2
    dma = pltpu.SemaphoreType.DMA
    return pl.pallas_call(
        functools.partial(gather_kernel, chips),
        out_shape=jax.ShapeDtypeStruct((count,) + shard.shape, shard.dtype),
        in_specs=[pl.BlockSpec(memory_space=pl.ANY)],
        out_specs=pl.BlockSpec(memory_space=pl.ANY),
        scratch_shapes=[
            dma((2, chips - 1)),
            dma((2, chips - 1)),
            dma((2, chips - 1)),
            dma((2, chips - 1)),
            dma(()),
            dma(()),
            dma(()),
        ],
        compiler_params=pltpu.CompilerParams(collective_id=0, has_side_effects=True),
        name="gather_weights",
    )(shard)


def scatter_kernel(chips, parts, total, own, paired, staged, landed, local_sem, pair_send, pair_recv, ring_send, ring_recv):
    place, core = own_place(chips)
    width = total.shape[1] // 2
    right = device_at((place + 1) % chips, core, chips)
    left = device_at((place + chips - 1) % chips, core, chips)
    sibling = device_at(place, 1 - core, chips)
    meet(right, left, sibling)
    pairs = [[None, None] for _ in range(chips)]
    keeps = [[None, None] for _ in range(chips)]
    for hop in range(chips):
        for way in range(2):
            columns = pl.ds(way * width, width)
            shift = (1 + hop) if way == 1 else (2 * chips - 1 - hop)
            owner = (place + shift) % chips
            pair = remote(
                parts.at[device_at(owner, 1 - core, chips), :, columns],
                paired.at[way, hop],
                pair_send.at[way, hop],
                pair_recv.at[way, hop],
                sibling,
            )
            pair.start()
            pairs[hop][way] = pair
            keep = pltpu.make_async_copy(
                parts.at[device_at(owner, core, chips), :, columns],
                own.at[way, hop],
                local_sem.at[way, hop],
            )
            keep.start()
            keeps[hop][way] = keep
    copies = []
    for hop in range(chips):
        started = []
        for way in range(2):
            columns = pl.ds(way * width, width)
            keeps[hop][way].wait()
            pairs[hop][way].wait_recv()
            value = own[way, hop].astype(jnp.float32) + paired[way, hop].astype(jnp.float32)
            if hop > 0:
                copies[hop - 1][way].wait_recv()
                value = value + landed[way, hop - 1].astype(jnp.float32)
            if hop < chips - 1:
                staged[way, hop] = value.astype(staged.dtype)
                copy = remote(
                    staged.at[way, hop],
                    landed.at[way, hop],
                    ring_send.at[way, hop],
                    ring_recv.at[way, hop],
                    left if way == 1 else right,
                )
                copy.start()
                started.append(copy)
            else:
                total[:, columns] = value
        copies.append(started)
    for started in copies:
        for copy in started:
            copy.wait_send()
    for hop in range(chips):
        for way in range(2):
            pairs[hop][way].wait_send()


def scatter_sum(parts):
    count, rows, columns = parts.shape
    chips = count // 2
    dma = pltpu.SemaphoreType.DMA
    width = columns // 2
    return pl.pallas_call(
        functools.partial(scatter_kernel, chips),
        out_shape=jax.ShapeDtypeStruct((rows, columns), jnp.float32),
        in_specs=[pl.BlockSpec(memory_space=pl.ANY)],
        out_specs=pl.BlockSpec(memory_space=pltpu.VMEM),
        scratch_shapes=[
            pltpu.VMEM((2, chips, rows, width), parts.dtype),
            pltpu.VMEM((2, chips, rows, width), parts.dtype),
            pltpu.VMEM((2, chips - 1, rows, width), parts.dtype),
            pltpu.VMEM((2, chips - 1, rows, width), parts.dtype),
            dma((2, chips)),
            dma((2, chips)),
            dma((2, chips)),
            dma((2, chips - 1)),
            dma((2, chips - 1)),
        ],
        compiler_params=pltpu.CompilerParams(collective_id=1, has_side_effects=True),
        name="scatter_grads",
    )(parts)


def pack_rows(qkv_part, out_part, in_part, down_part, gain_rows):
    rows = qkv_part.shape[-2]
    spare = 2 * rows - down_part.shape[-2]
    tail = jnp.concatenate(
        [
            down_part[..., rows:, :],
            jnp.pad(
                gain_rows,
                [(0, 0)] * (gain_rows.ndim - 2)
                + [(0, spare - 2), (0, down_part.shape[-1] - gain_rows.shape[-1])],
            ),
        ],
        axis=-2,
    )
    return jnp.concatenate([qkv_part, out_part, in_part, down_part[..., :rows, :], tail], axis=-1)


def unpack_rows(packed, model_width, hidden, hidden_share):
    rows = packed.shape[-2]
    rest = hidden_share - rows
    first = 3 * model_width
    second = first + model_width
    third = second + 2 * hidden
    fourth = third + model_width
    down_part = jnp.concatenate(
        [packed[..., third:fourth], packed[..., :rest, fourth:]], axis=-2
    )
    gain_rows = packed[..., rest : rest + 2, fourth : fourth + rows]
    return (
        packed[..., :first],
        packed[..., first:second],
        packed[..., second:third],
        down_part,
        gain_rows,
    )


def body(tokens, cotangent, lengths, w_qkv, w_out, w_in, w_down, gain_attn, gain_mlp):
    section_index = lax.axis_index("section")
    first_section = section_index == 0
    micro_count = lengths.shape[0]
    row_count = tokens.shape[0] // micro_count
    model_width = tokens.shape[1]
    device_count = lax.axis_size("dp")
    feature_share = w_qkv.shape[1]
    hidden_share = w_down.shape[1]
    hidden = hidden_share * device_count
    token_blocks = tokens.reshape(micro_count, row_count, model_width)
    cotangent_blocks = cotangent.reshape(micro_count, row_count, model_width)
    rope_base = jnp.where(first_section, 10000.0, 160000.0).astype(jnp.float32)
    window_reach = jnp.where(first_section, WINDOW, row_count).astype(jnp.int32)
    packed = pack_rows(
        w_qkv[0], w_out[0], w_in[0], w_down[0], jnp.concatenate([gain_attn, gain_mlp], axis=0)
    )
    gathered = unpack_rows(gather_all(packed), model_width, hidden, hidden_share)
    weights = tuple(
        (member.reshape(-1, member.shape[-1]) for member in gathered[:4])
    ) + (gathered[4][:, 0].reshape(-1), gathered[4][:, 1].reshape(-1))

    received = jnp.zeros((row_count, model_width), jnp.bfloat16)
    kept_list = []
    out_list = []
    for tick_index in range(micro_count + 1):
        block_index = jnp.clip(tick_index - section_index, 0, micro_count - 1)
        lengths_row = lax.dynamic_index_in_dim(lengths, block_index, 0, keepdims=False)
        own_block = token_blocks[min(tick_index, micro_count - 1)]
        inputs_b = jnp.where(first_section, own_block, received)
        result, kept_state = layer_forward(inputs_b, weights, lengths_row, window_reach, rope_base)
        kept_list.append(kept_state)
        out_list.append(result)
        if tick_index < micro_count:
            received = from_behind(result, "section", 1)

    layer_out = jnp.concatenate(
        [
            jnp.where(first_section, out_list[index], out_list[index + 1])
            for index in range(micro_count)
        ]
    )[None]
    kept_rows = [
        jax.tree.map(
            lambda early, late: jnp.where(first_section, early, late),
            kept_list[index],
            kept_list[index + 1],
        )
        for index in range(micro_count)
    ]

    received_grad = jnp.zeros((row_count, model_width), jnp.bfloat16)
    grad_list = []
    extra_list = []
    for tick_index in range(micro_count + 1):
        early, late = max(tick_index - 1, 0), min(tick_index, micro_count - 1)
        kept_state = jax.tree.map(
            lambda one, other: jnp.where(first_section, one, other),
            kept_rows[early],
            kept_rows[late],
        )
        own_cot = cotangent_blocks[late]
        upstream_b = jnp.where(first_section, received_grad, own_cot)
        d_input, extras = layer_backward(upstream_b, kept_state, weights, window_reach, rope_base)
        grad_list.append(d_input)
        extra_list.append(extras)
        if tick_index < micro_count:
            received_grad = from_behind(d_input, "section", -1)

    def pick_backward(columns):
        return [
            jnp.where(first_section, columns[index + 1], columns[index])
            for index in range(micro_count)
        ]

    input_grad = jnp.concatenate(pick_backward(grad_list))[None]
    ln_first, attended, ln_second, geglu_out = [
        jnp.concatenate([kept[slot] for kept in kept_rows]) for slot in (0, 7, 10, 12)
    ]
    d_projected, d_middle_b, d_up, upstream_b = [
        jnp.concatenate(pick_backward([extras[slot] for extras in extra_list])) for slot in range(4)
    ]
    attn_gain_grad, mlp_gain_grad = [
        functools.reduce(jnp.add, pick_backward([extras[slot] for extras in extra_list]))
        for slot in (4, 5)
    ]

    def weight_grad(left_side, right_side, share):
        product = contract("rc,rf->cf", left_side, right_side).astype(jnp.bfloat16)
        return product.reshape(device_count, share, product.shape[-1])

    gain_rows = jnp.stack(
        [
            attn_gain_grad.reshape(device_count, feature_share),
            mlp_gain_grad.reshape(device_count, feature_share),
        ],
        axis=1,
    ).astype(jnp.bfloat16)
    parts = pack_rows(
        weight_grad(ln_first, d_projected, feature_share),
        weight_grad(attended, d_middle_b, feature_share),
        weight_grad(ln_second, d_up, feature_share),
        weight_grad(geglu_out, upstream_b, hidden_share),
        gain_rows,
    )
    qkv_grad, out_grad, in_grad, down_grad, gain_grads = unpack_rows(
        scatter_sum(parts), model_width, hidden, hidden_share
    )
    return (
        layer_out,
        input_grad,
        qkv_grad[None],
        out_grad[None],
        in_grad[None],
        down_grad[None],
        gain_grads[0:1],
        gain_grads[1:2],
    )


def solution(mesh):
    return jax.shard_map(
        body,
        mesh=mesh,
        in_specs=(
            P("dp", None),
            P("dp", None),
            P("dp", None),
            P("section", "dp", None),
            P("section", "dp", None),
            P("section", "dp", None),
            P("section", "dp", None),
            P("section", "dp"),
            P("section", "dp"),
        ),
        out_specs=(
            P("section", "dp", None),
            P("section", "dp", None),
            P("section", "dp", None),
            P("section", "dp", None),
            P("section", "dp", None),
            P("section", "dp", None),
            P("section", "dp"),
            P("section", "dp"),
        ),
        check_vma=False,
    )
```

```python
import functools
import math

import jax
import jax.numpy as jnp
from jax import lax
from jax.experimental import pallas as pl
from jax.experimental.pallas import tpu as pltpu
from jax.sharding import PartitionSpec as P

HEAD_DIM = 64
WINDOW = 64


norm_epsilon = 1e-05


def from_behind(value, axis, steps):
    count = lax.axis_size(axis)
    leading, last = (max(0, -steps), min(count, count - steps))
    return lax.ppermute(value, axis, [(source, source + steps) for source in range(leading, last)])


def contract(formula, left_side, right_side):
    return jnp.einsum(formula, left_side, right_side, preferred_element_type=jnp.float32)


def pack_layout(lengths_row, row_count, window_reach):
    row_ids = jnp.arange(row_count, dtype=jnp.int32)
    doc_ends = jnp.cumsum(lengths_row)
    passed = row_ids[:, None] >= doc_ends[None, :]
    doc_ids = jnp.sum(passed.astype(jnp.int32), axis=1)
    starts = jnp.max(jnp.where(passed, doc_ends[None, :], 0), axis=1)
    positions = row_ids - starts
    allowed = (doc_ids[:, None] == doc_ids[None, :]) & (
        jnp.abs(row_ids[:, None] - row_ids[None, :]) <= window_reach
    )
    return (allowed, positions)


def rotation(positions, rope_base):
    half_dim = HEAD_DIM // 2
    frequency = jnp.exp(
        -jnp.log(rope_base) * (2.0 * jnp.arange(half_dim, dtype=jnp.float32) / HEAD_DIM)
    )
    angles = positions.astype(jnp.float32)[:, None] * frequency[None, :]
    return (jnp.cos(angles)[:, None, :], jnp.sin(angles)[:, None, :])


def normalize(values):
    centered = values - jnp.mean(values, axis=-1, keepdims=True)
    inverse = lax.rsqrt(jnp.mean(centered * centered, axis=-1, keepdims=True) + norm_epsilon)
    return (centered * inverse, inverse)


def norm_backward(upstream, gain_row, normed, inverse):
    scaled = upstream * gain_row
    return inverse * (
        scaled
        - jnp.mean(scaled, axis=-1, keepdims=True)
        - normed * jnp.mean(scaled * normed, axis=-1, keepdims=True)
    )


def swap_halves(values):
    half = HEAD_DIM // 2
    width = values.shape[1]
    lanes = lax.broadcasted_iota(jnp.int32, values.shape, 1)
    return jnp.where(
        lanes % HEAD_DIM < half,
        pltpu.roll(values, width - half, 1),
        pltpu.roll(values, half, 1),
    )


def widen(table, width):
    return jnp.concatenate([table] * (width // table.shape[1]), axis=1)


def dot_nn(left_side, right_side):
    return lax.dot_general(
        left_side, right_side, (((1,), (0,)), ((), ())), preferred_element_type=jnp.float32
    )


def dot_nt(left_side, right_side):
    return lax.dot_general(
        left_side, right_side, (((1,), (1,)), ((), ())), preferred_element_type=jnp.float32
    )


def dot_tn(left_side, right_side):
    return lax.dot_general(
        left_side, right_side, (((0,), (0,)), ((), ())), preferred_element_type=jnp.float32
    )


def normal_below(values):
    return 0.5 * (1.0 + lax.erf(values * (0.5**0.5)))


KEPT = 10


def forward_kernel(scalars, tokens, received, bias, cosine, sine_part, wide, down, gains, *refs):
    result, layer_out, kept_x, kept_ln, kept_qkv, kept_probs, kept_attn, kept_mid, kept_ln2, kept_up, kept_geglu = refs[-KEPT - 1 :]
    width = tokens.shape[-1]
    hidden = down.shape[0]
    heads = width // HEAD_DIM
    inputs_b = jnp.where(scalars[1] == 0, tokens[0], received[...])
    kept_x[0] = inputs_b
    residual = inputs_b.astype(jnp.float32)
    normed, _ = normalize(residual)
    ln_first = (normed * gains[0:1, :]).astype(jnp.bfloat16)
    kept_ln[0] = ln_first
    projected = dot_nn(ln_first, wide[:, : 3 * width])
    cosines = widen(cosine[0], width)
    sines = widen(sine_part[0], width)
    for part in range(2):
        piece = projected[:, part * width : (part + 1) * width]
        kept_qkv[0, :, part * width : (part + 1) * width] = (
            piece * cosines + swap_halves(piece) * sines
        ).astype(jnp.bfloat16)
    kept_qkv[0, :, 2 * width :] = projected[:, 2 * width :].astype(jnp.bfloat16)
    attended = []
    for head in range(heads):
        at = head * HEAD_DIM
        queries = kept_qkv[0, :, at : at + HEAD_DIM]
        keys_rot = kept_qkv[0, :, width + at : width + at + HEAD_DIM]
        values_b = kept_qkv[0, :, 2 * width + at : 2 * width + at + HEAD_DIM]
        scores = jnp.where(
            bias[0] > 0, dot_nt(queries, keys_rot) * (1.0 / HEAD_DIM**0.5), -1e30
        )
        shifted = scores - jnp.max(scores, axis=-1, keepdims=True)
        powers = jnp.exp(shifted)
        probs = powers / jnp.sum(powers, axis=-1, keepdims=True)
        kept_probs[0, head] = probs
        attended.append(dot_nn(probs.astype(jnp.bfloat16), values_b))
    attended = jnp.concatenate(attended, axis=1).astype(jnp.bfloat16)
    kept_attn[0] = attended
    middle = residual + dot_nn(attended, wide[:, 3 * width : 4 * width])
    kept_mid[0] = middle
    normed, _ = normalize(middle)
    ln_second = (normed * gains[1:2, :]).astype(jnp.bfloat16)
    kept_ln2[0] = ln_second
    upward = dot_nn(ln_second, wide[:, 4 * width : 4 * width + 2 * hidden])
    kept_up[0] = upward
    gate = upward[:, :hidden]
    geglu = (gate * normal_below(gate) * upward[:, hidden:]).astype(jnp.bfloat16)
    kept_geglu[0] = geglu
    outcome = (middle + dot_nn(geglu, down[...])).astype(jnp.bfloat16)
    result[...] = outcome
    layer_out[0] = outcome


def backward_kernel(
    scalars, cotangent, received, cosine, sine_part, wide, down, gains,
    kept_x, kept_qkv, kept_probs, kept_mid, kept_up, *refs
):
    result, input_grad, kept_dy, kept_dup, kept_dmid, kept_dqkv, gain_grads = refs[-7:]
    width = cotangent.shape[-1]
    hidden = down.shape[0]
    heads = width // HEAD_DIM
    upstream_b = jnp.where(scalars[1] == 0, received[...], cotangent[0])
    kept_dy[0] = upstream_b
    d_geglu = dot_nt(upstream_b, down[...])
    gate = kept_up[0, :, :hidden]
    below = normal_below(gate)
    slope = below + gate * jnp.exp(-0.5 * gate * gate) * (2.0 * math.pi) ** -0.5
    kept_dup[0, :, :hidden] = (d_geglu * kept_up[0, :, hidden:] * slope).astype(jnp.bfloat16)
    kept_dup[0, :, hidden:] = (d_geglu * (gate * below)).astype(jnp.bfloat16)
    d_ln_second = dot_nt(kept_dup[0], wide[:, 4 * width : 4 * width + 2 * hidden])
    normed, inverse = normalize(kept_mid[0])
    gain_grads[0, 1:2, :] = jnp.sum(d_ln_second * normed, axis=0, keepdims=True)
    d_middle = upstream_b.astype(jnp.float32) + norm_backward(
        d_ln_second, gains[1:2, :], normed, inverse
    )
    d_middle_b = d_middle.astype(jnp.bfloat16)
    kept_dmid[0] = d_middle_b
    d_attended = dot_nt(d_middle_b, wide[:, 3 * width : 4 * width]).astype(jnp.bfloat16)
    d_queries, d_keys, d_values = [], [], []
    for head in range(heads):
        at = head * HEAD_DIM
        queries = kept_qkv[0, :, at : at + HEAD_DIM]
        keys_rot = kept_qkv[0, :, width + at : width + at + HEAD_DIM]
        values_b = kept_qkv[0, :, 2 * width + at : 2 * width + at + HEAD_DIM]
        d_out = d_attended[:, at : at + HEAD_DIM]
        probs = kept_probs[0, head]
        d_values.append(dot_tn(probs.astype(jnp.bfloat16), d_out))
        d_probs = dot_nt(d_out, values_b)
        row_delta = jnp.sum(probs * d_probs, axis=-1, keepdims=True)
        d_scores = (probs * (d_probs - row_delta)).astype(jnp.bfloat16)
        d_queries.append(dot_nn(d_scores, keys_rot))
        d_keys.append(dot_tn(d_scores, queries))
    cosines = widen(cosine[0], width)
    sines = widen(sine_part[0], width)
    for part, pieces in enumerate((d_queries, d_keys)):
        piece = jnp.concatenate(pieces, axis=1) * (1.0 / HEAD_DIM**0.5)
        kept_dqkv[0, :, part * width : (part + 1) * width] = (
            piece * cosines - swap_halves(piece) * sines
        ).astype(jnp.bfloat16)
    kept_dqkv[0, :, 2 * width :] = jnp.concatenate(d_values, axis=1).astype(jnp.bfloat16)
    d_ln_first = dot_nt(kept_dqkv[0], wide[:, : 3 * width])
    normed, inverse = normalize(kept_x[0].astype(jnp.float32))
    gain_grads[0, 0:1, :] = jnp.sum(d_ln_first * normed, axis=0, keepdims=True)
    outcome = (
        d_middle + norm_backward(d_ln_first, gains[0:1, :], normed, inverse)
    ).astype(jnp.bfloat16)
    result[...] = outcome
    input_grad[0] = outcome


def stage(kernel, name, scalars, blocked, whole, slot_shapes, result_shape, carried):
    def blocked_spec(shape):
        rank = len(shape)
        return pl.BlockSpec(
            (1,) + tuple(shape[1:]), lambda step, picked: (picked[0],) + (0,) * (rank - 1)
        )

    def whole_spec(shape):
        rank = len(shape)
        return pl.BlockSpec(
            tuple(shape), lambda step, picked: (0,) * rank, pipeline_mode=pl.Buffered(1)
        )

    operands, specs = [], []
    for kind, operand in zip(blocked, whole):
        operands.append(operand)
        specs.append(blocked_spec(operand.shape) if kind else whole_spec(operand.shape))
    aliases = {}
    if carried is not None:
        for offset, operand in enumerate(carried):
            aliases[1 + len(operands)] = 1 + offset
            operands.append(operand)
            specs.append(pl.BlockSpec(memory_space=pl.ANY))
    outcome = pl.pallas_call(
        kernel,
        grid_spec=pltpu.PrefetchScalarGridSpec(
            num_scalar_prefetch=1,
            grid=(1,),
            in_specs=specs,
            out_specs=[whole_spec(result_shape.shape)]
            + [blocked_spec(shape.shape) for shape in slot_shapes],
        ),
        out_shape=[result_shape] + list(slot_shapes),
        input_output_aliases=aliases,
        compiler_params=pltpu.CompilerParams(vmem_limit_bytes=60000 * 1024),
        name=name,
    )(scalars, *operands)
    return outcome[0], outcome[1:]


def device_at(ring_place, core, chips):
    half = ring_place // (chips // 2)
    chip = (1 - half) * 2 * ring_place + half * (2 * (chips - 1 - ring_place) + 1)
    return chip * 2 + core


def own_place(chips):
    index = lax.axis_index("dp")
    chip = index // 2
    column = chip % 2
    depth = chip // 2
    return ((1 - column) * depth + column * (chips - 1 - depth), index % 2)


def meet(right, left, sibling):
    barrier = pltpu.get_barrier_semaphore()
    for partner in (right, left, sibling):
        pl.semaphore_signal(
            barrier, inc=1, device_id={"dp": partner}, device_id_type=pl.DeviceIdType.MESH
        )
    pl.semaphore_wait(barrier, 3)


def remote(source, target, send_sem, recv_sem, partner):
    return pltpu.make_async_remote_copy(
        src_ref=source,
        dst_ref=target,
        send_sem=send_sem,
        recv_sem=recv_sem,
        device_id={"dp": partner},
        device_id_type=pl.DeviceIdType.MESH,
    )


def gather_kernel(chips, shard, full, ring_send, ring_recv, pair_send, pair_recv, own_send, own_recv, local_sem):
    place, core = own_place(chips)
    width = shard.shape[1] // 2
    right = device_at((place + 1) % chips, core, chips)
    left = device_at((place + chips - 1) % chips, core, chips)
    index = device_at(place, core, chips)
    sibling = device_at(place, 1 - core, chips)
    meet(right, left, sibling)
    keep = pltpu.make_async_copy(shard, full.at[index], local_sem)
    keep.start()
    waiting = []
    ring_copies = []
    for step in range(chips - 1):
        started = []
        for way in range(2):
            columns = pl.ds(way * width, width)
            shift = step if way == 1 else chips - step
            block = device_at((place + shift) % chips, core, chips)
            source = shard.at[:, columns] if step == 0 else full.at[block, :, columns]
            if step > 0:
                ring_copies[step - 1][way].wait_recv()
            copy = remote(
                source,
                full.at[block, :, columns],
                ring_send.at[way, step],
                ring_recv.at[way, step],
                left if way == 1 else right,
            )
            copy.start()
            started.append(copy)
            if step > 0:
                pair = remote(
                    source,
                    full.at[block, :, columns],
                    pair_send.at[way, step - 1],
                    pair_recv.at[way, step - 1],
                    sibling,
                )
                pair.start()
                waiting.append(pair)
        if step == 0:
            pair = remote(shard, full.at[index], own_send, own_recv, sibling)
            pair.start()
            waiting.append(pair)
        ring_copies.append(started)
    for way in range(2):
        ring_copies[-1][way].wait_recv()
        columns = pl.ds(way * width, width)
        shift = chips - 1 if way == 1 else 1
        block = device_at((place + shift) % chips, core, chips)
        pair = remote(
            full.at[block, :, columns],
            full.at[block, :, columns],
            pair_send.at[way, chips - 2],
            pair_recv.at[way, chips - 2],
            sibling,
        )
        pair.start()
        waiting.append(pair)
    for started in ring_copies:
        for copy in started:
            copy.wait_send()
    for pair in waiting:
        pair.wait()
    keep.wait()


def gather_all(shard):
    count = lax.axis_size("dp")
    chips = count // 2
    dma = pltpu.SemaphoreType.DMA
    return pl.pallas_call(
        functools.partial(gather_kernel, chips),
        out_shape=jax.ShapeDtypeStruct((count,) + shard.shape, shard.dtype),
        in_specs=[pl.BlockSpec(memory_space=pl.ANY)],
        out_specs=pl.BlockSpec(memory_space=pl.ANY),
        scratch_shapes=[
            dma((2, chips - 1)),
            dma((2, chips - 1)),
            dma((2, chips - 1)),
            dma((2, chips - 1)),
            dma(()),
            dma(()),
            dma(()),
        ],
        compiler_params=pltpu.CompilerParams(collective_id=0, has_side_effects=True),
        name="gather_weights",
    )(shard)


def scatter_kernel(chips, parts, total, own, paired, staged, landed, local_sem, pair_send, pair_recv, ring_send, ring_recv):
    place, core = own_place(chips)
    width = total.shape[1] // 2
    right = device_at((place + 1) % chips, core, chips)
    left = device_at((place + chips - 1) % chips, core, chips)
    sibling = device_at(place, 1 - core, chips)
    meet(right, left, sibling)
    pairs = [[None, None] for _ in range(chips)]
    keeps = [[None, None] for _ in range(chips)]
    for hop in range(chips):
        for way in range(2):
            columns = pl.ds(way * width, width)
            shift = (1 + hop) if way == 1 else (2 * chips - 1 - hop)
            owner = (place + shift) % chips
            pair = remote(
                parts.at[device_at(owner, 1 - core, chips), :, columns],
                paired.at[way, hop],
                pair_send.at[way, hop],
                pair_recv.at[way, hop],
                sibling,
            )
            pair.start()
            pairs[hop][way] = pair
            keep = pltpu.make_async_copy(
                parts.at[device_at(owner, core, chips), :, columns],
                own.at[way, hop],
                local_sem.at[way, hop],
            )
            keep.start()
            keeps[hop][way] = keep
    copies = []
    for hop in range(chips):
        started = []
        for way in range(2):
            columns = pl.ds(way * width, width)
            keeps[hop][way].wait()
            pairs[hop][way].wait_recv()
            value = own[way, hop].astype(jnp.float32) + paired[way, hop].astype(jnp.float32)
            if hop > 0:
                copies[hop - 1][way].wait_recv()
                value = value + landed[way, hop - 1].astype(jnp.float32)
            if hop < chips - 1:
                staged[way, hop] = value.astype(staged.dtype)
                copy = remote(
                    staged.at[way, hop],
                    landed.at[way, hop],
                    ring_send.at[way, hop],
                    ring_recv.at[way, hop],
                    left if way == 1 else right,
                )
                copy.start()
                started.append(copy)
            else:
                total[:, columns] = value
        copies.append(started)
    for started in copies:
        for copy in started:
            copy.wait_send()
    for hop in range(chips):
        for way in range(2):
            pairs[hop][way].wait_send()


def scatter_sum(parts):
    count, rows, columns = parts.shape
    chips = count // 2
    dma = pltpu.SemaphoreType.DMA
    width = columns // 2
    return pl.pallas_call(
        functools.partial(scatter_kernel, chips),
        out_shape=jax.ShapeDtypeStruct((rows, columns), jnp.float32),
        in_specs=[pl.BlockSpec(memory_space=pl.ANY)],
        out_specs=pl.BlockSpec(memory_space=pltpu.VMEM),
        scratch_shapes=[
            pltpu.VMEM((2, chips, rows, width), parts.dtype),
            pltpu.VMEM((2, chips, rows, width), parts.dtype),
            pltpu.VMEM((2, chips - 1, rows, width), parts.dtype),
            pltpu.VMEM((2, chips - 1, rows, width), parts.dtype),
            dma((2, chips)),
            dma((2, chips)),
            dma((2, chips)),
            dma((2, chips - 1)),
            dma((2, chips - 1)),
        ],
        compiler_params=pltpu.CompilerParams(collective_id=1, has_side_effects=True),
        name="scatter_grads",
    )(parts)


def pack_rows(qkv_part, out_part, in_part, down_part, gain_rows):
    rows = qkv_part.shape[-2]
    spare = 2 * rows - down_part.shape[-2]
    tail = jnp.concatenate(
        [
            down_part[..., rows:, :],
            jnp.pad(
                gain_rows,
                [(0, 0)] * (gain_rows.ndim - 2)
                + [(0, spare - 2), (0, down_part.shape[-1] - gain_rows.shape[-1])],
            ),
        ],
        axis=-2,
    )
    return jnp.concatenate([qkv_part, out_part, in_part, down_part[..., :rows, :], tail], axis=-1)


def unpack_rows(packed, model_width, hidden, hidden_share):
    rows = packed.shape[-2]
    rest = hidden_share - rows
    first = 3 * model_width
    second = first + model_width
    third = second + 2 * hidden
    fourth = third + model_width
    down_part = jnp.concatenate(
        [packed[..., third:fourth], packed[..., :rest, fourth:]], axis=-2
    )
    gain_rows = packed[..., rest : rest + 2, fourth : fourth + rows]
    return (
        packed[..., :first],
        packed[..., first:second],
        packed[..., second:third],
        down_part,
        gain_rows,
    )


def body(tokens, cotangent, lengths, w_qkv, w_out, w_in, w_down, gain_attn, gain_mlp):
    section_index = lax.axis_index("section")
    first_section = section_index == 0
    micro_count = lengths.shape[0]
    row_count = tokens.shape[0] // micro_count
    model_width = tokens.shape[1]
    device_count = lax.axis_size("dp")
    feature_share = w_qkv.shape[1]
    hidden_share = w_down.shape[1]
    hidden = hidden_share * device_count
    token_blocks = tokens.reshape(micro_count, row_count, model_width)
    cotangent_blocks = cotangent.reshape(micro_count, row_count, model_width)
    rope_base = jnp.where(first_section, 10000.0, 160000.0).astype(jnp.float32)
    window_reach = jnp.where(first_section, WINDOW, row_count).astype(jnp.int32)
    packed = pack_rows(
        w_qkv[0], w_out[0], w_in[0], w_down[0], jnp.concatenate([gain_attn, gain_mlp], axis=0)
    )
    allowed, positions = jax.vmap(lambda row: pack_layout(row, row_count, window_reach))(lengths)
    allowed = allowed.astype(jnp.float32)
    cosine, sine_part = jax.vmap(lambda places: rotation(places, rope_base))(positions)
    cosine, sine_part = cosine[:, :, 0], sine_part[:, :, 0]
    cosine = jnp.concatenate([cosine] * 4, axis=-1)
    sine_part = jnp.concatenate([-sine_part, sine_part] * 2, axis=-1)
    packed, allowed, cosine, sine_part = lax.optimization_barrier(
        (packed, allowed, cosine, sine_part)
    )
    gathered = gather_all(packed)
    wide = gathered.reshape(-1, gathered.shape[-1])
    down_part, gain_rows = unpack_rows(gathered, model_width, hidden, hidden_share)[3:]
    down = down_part.reshape(hidden, model_width)
    gains = jnp.swapaxes(gain_rows, 0, 1).reshape(2, model_width).astype(jnp.float32)

    def slots(columns, kind=jnp.bfloat16):
        return jax.ShapeDtypeStruct((micro_count, row_count, columns), kind)

    heads = model_width // HEAD_DIM
    block_shape = jax.ShapeDtypeStruct((row_count, model_width), jnp.bfloat16)
    forward_shapes = [
        slots(model_width),
        slots(model_width),
        slots(model_width),
        slots(3 * model_width),
        jax.ShapeDtypeStruct((micro_count, heads, row_count, row_count), jnp.float32),
        slots(model_width),
        slots(model_width, jnp.float32),
        slots(model_width),
        slots(2 * hidden, jnp.float32),
        slots(hidden),
    ]
    received = token_blocks[0]
    kept = None
    for tick_index in range(micro_count + 1):
        slot = jnp.clip(tick_index - section_index, 0, micro_count - 1)
        scalars = jnp.stack([slot, section_index]).astype(jnp.int32)
        result, kept = stage(
            forward_kernel,
            "forward_tick",
            scalars,
            (True, False, True, True, True, False, False, False),
            (token_blocks, received, allowed, cosine, sine_part, wide, down, gains),
            forward_shapes,
            block_shape,
            kept,
        )
        if tick_index < micro_count:
            received = from_behind(result, "section", 1)
    layer_out, inputs_b, ln_first, qkv, probs, attended, middle, ln_second, upward, geglu = kept

    backward_shapes = [
        slots(model_width),
        slots(model_width),
        slots(2 * hidden),
        slots(model_width),
        slots(3 * model_width),
        jax.ShapeDtypeStruct((micro_count, 2, model_width), jnp.float32),
    ]
    received = cotangent_blocks[0]
    kept = None
    for tick_index in range(micro_count + 1):
        slot = jnp.clip(tick_index + section_index - 1, 0, micro_count - 1)
        scalars = jnp.stack([slot, section_index]).astype(jnp.int32)
        result, kept = stage(
            backward_kernel,
            "backward_tick",
            scalars,
            (True, False, True, True, False, False, False, True, True, True, True, True),
            (
                cotangent_blocks, received, cosine, sine_part, wide, down, gains,
                inputs_b, qkv, probs, middle, upward,
            ),
            backward_shapes,
            block_shape,
            kept,
        )
        if tick_index < micro_count:
            received = from_behind(result, "section", -1)
    input_grad, d_out, d_up, d_mid, d_qkv, gain_grads = kept

    def rows_of(slotted):
        return slotted.reshape(micro_count * row_count, slotted.shape[-1])

    def weight_grad(left_side, right_side, share):
        product = contract("rc,rf->cf", rows_of(left_side), rows_of(right_side)).astype(
            jnp.bfloat16
        )
        return product.reshape(device_count, share, product.shape[-1])

    gain_rows = jnp.swapaxes(
        jnp.sum(gain_grads, axis=0).reshape(2, device_count, feature_share), 0, 1
    ).astype(jnp.bfloat16)
    parts = pack_rows(
        weight_grad(ln_first, d_qkv, feature_share),
        weight_grad(attended, d_mid, feature_share),
        weight_grad(ln_second, d_up, feature_share),
        weight_grad(geglu, d_out, hidden_share),
        gain_rows,
    )
    qkv_grad, out_grad, in_grad, down_grad, gain_sums = unpack_rows(
        scatter_sum(parts), model_width, hidden, hidden_share
    )
    return (
        layer_out.reshape(1, micro_count * row_count, model_width),
        input_grad.reshape(1, micro_count * row_count, model_width),
        qkv_grad[None],
        out_grad[None],
        in_grad[None],
        down_grad[None],
        gain_sums[0:1],
        gain_sums[1:2],
    )


def solution(mesh):
    return jax.shard_map(
        body,
        mesh=mesh,
        in_specs=(
            P("dp", None),
            P("dp", None),
            P("dp", None),
            P("section", "dp", None),
            P("section", "dp", None),
            P("section", "dp", None),
            P("section", "dp", None),
            P("section", "dp"),
            P("section", "dp"),
        ),
        out_specs=(
            P("section", "dp", None),
            P("section", "dp", None),
            P("section", "dp", None),
            P("section", "dp", None),
            P("section", "dp", None),
            P("section", "dp", None),
            P("section", "dp"),
            P("section", "dp"),
        ),
        check_vma=False,
    )
```

```python
import functools
import math

import jax
import jax.numpy as jnp
from jax import lax
from jax.experimental import pallas as pl
from jax.experimental.pallas import tpu as pltpu
from jax.sharding import PartitionSpec as P

HEAD_DIM = 64
WINDOW = 64


norm_epsilon = 1e-05


def from_behind(value, axis, steps):
    count = lax.axis_size(axis)
    leading, last = (max(0, -steps), min(count, count - steps))
    return lax.ppermute(value, axis, [(source, source + steps) for source in range(leading, last)])


def contract(formula, left_side, right_side):
    return jnp.einsum(formula, left_side, right_side, preferred_element_type=jnp.float32)


def pack_layout(lengths_row, row_count, window_reach):
    row_ids = jnp.arange(row_count, dtype=jnp.int32)
    doc_ends = jnp.cumsum(lengths_row)
    passed = row_ids[:, None] >= doc_ends[None, :]
    doc_ids = jnp.sum(passed.astype(jnp.int32), axis=1)
    starts = jnp.max(jnp.where(passed, doc_ends[None, :], 0), axis=1)
    positions = row_ids - starts
    allowed = (doc_ids[:, None] == doc_ids[None, :]) & (
        jnp.abs(row_ids[:, None] - row_ids[None, :]) <= window_reach
    )
    return (allowed, positions)


def rotation(positions, rope_base):
    half_dim = HEAD_DIM // 2
    frequency = jnp.exp(
        -jnp.log(rope_base) * (2.0 * jnp.arange(half_dim, dtype=jnp.float32) / HEAD_DIM)
    )
    angles = positions.astype(jnp.float32)[:, None] * frequency[None, :]
    return (jnp.cos(angles)[:, None, :], jnp.sin(angles)[:, None, :])


def normalize(values):
    centered = values - jnp.mean(values, axis=-1, keepdims=True)
    inverse = lax.rsqrt(jnp.mean(centered * centered, axis=-1, keepdims=True) + norm_epsilon)
    return (centered * inverse, inverse)


def norm_backward(upstream, gain_row, normed, inverse):
    scaled = upstream * gain_row
    return inverse * (
        scaled
        - jnp.mean(scaled, axis=-1, keepdims=True)
        - normed * jnp.mean(scaled * normed, axis=-1, keepdims=True)
    )


def swap_halves(values):
    half = HEAD_DIM // 2
    width = values.shape[1]
    lanes = lax.broadcasted_iota(jnp.int32, values.shape, 1)
    return jnp.where(
        lanes % HEAD_DIM < half,
        pltpu.roll(values, width - half, 1),
        pltpu.roll(values, half, 1),
    )


def widen(table, width):
    return jnp.concatenate([table] * (width // table.shape[1]), axis=1)


def dot_nn(left_side, right_side):
    return lax.dot_general(
        left_side, right_side, (((1,), (0,)), ((), ())), preferred_element_type=jnp.float32
    )


def dot_nt(left_side, right_side):
    return lax.dot_general(
        left_side, right_side, (((1,), (1,)), ((), ())), preferred_element_type=jnp.float32
    )


def dot_tn(left_side, right_side):
    return lax.dot_general(
        left_side, right_side, (((0,), (0,)), ((), ())), preferred_element_type=jnp.float32
    )


def normal_below(values):
    return 0.5 * (1.0 + lax.erf(values * (0.5**0.5)))


KEPT = 10


def forward_kernel(scalars, tokens, received, bias, cosine, sine_part, wide, down, gains, *refs):
    result, layer_out, kept_x, kept_ln, kept_qkv, kept_probs, kept_attn, kept_mid, kept_ln2, kept_up, kept_geglu = refs[-KEPT - 1 :]
    width = tokens.shape[-1]
    hidden = down.shape[0]
    heads = width // HEAD_DIM
    inputs_b = jnp.where(scalars[1] == 0, tokens[0], received[...])
    kept_x[0] = inputs_b
    residual = inputs_b.astype(jnp.float32)
    normed, _ = normalize(residual)
    ln_first = (normed * gains[0:1, :]).astype(jnp.bfloat16)
    kept_ln[0] = ln_first
    projected = dot_nn(ln_first, wide[:, : 3 * width])
    cosines = widen(cosine[0], width)
    sines = widen(sine_part[0], width)
    for part in range(2):
        piece = projected[:, part * width : (part + 1) * width]
        kept_qkv[0, :, part * width : (part + 1) * width] = (
            piece * cosines + swap_halves(piece) * sines
        ).astype(jnp.bfloat16)
    kept_qkv[0, :, 2 * width :] = projected[:, 2 * width :].astype(jnp.bfloat16)
    attended = []
    for head in range(heads):
        at = head * HEAD_DIM
        queries = kept_qkv[0, :, at : at + HEAD_DIM]
        keys_rot = kept_qkv[0, :, width + at : width + at + HEAD_DIM]
        values_b = kept_qkv[0, :, 2 * width + at : 2 * width + at + HEAD_DIM]
        scores = jnp.where(
            bias[0] > 0, dot_nt(queries, keys_rot) * (1.0 / HEAD_DIM**0.5), -1e30
        )
        shifted = scores - jnp.max(scores, axis=-1, keepdims=True)
        powers = jnp.exp(shifted)
        probs = powers / jnp.sum(powers, axis=-1, keepdims=True)
        kept_probs[0, head] = probs
        attended.append(dot_nn(probs.astype(jnp.bfloat16), values_b))
    attended = jnp.concatenate(attended, axis=1).astype(jnp.bfloat16)
    kept_attn[0] = attended
    middle = residual + dot_nn(attended, wide[:, 3 * width : 4 * width])
    kept_mid[0] = middle
    normed, _ = normalize(middle)
    ln_second = (normed * gains[1:2, :]).astype(jnp.bfloat16)
    kept_ln2[0] = ln_second
    upward = dot_nn(ln_second, wide[:, 4 * width : 4 * width + 2 * hidden])
    kept_up[0] = upward
    gate = upward[:, :hidden]
    geglu = (gate * normal_below(gate) * upward[:, hidden:]).astype(jnp.bfloat16)
    kept_geglu[0] = geglu
    outcome = (middle + dot_nn(geglu, down[...])).astype(jnp.bfloat16)
    result[...] = outcome
    layer_out[0] = outcome


def backward_kernel(
    scalars, cotangent, received, cosine, sine_part, wide, down, gains,
    kept_x, kept_qkv, kept_probs, kept_mid, kept_up, *refs
):
    result, input_grad, kept_dy, kept_dup, kept_dmid, kept_dqkv, gain_grads = refs[-7:]
    width = cotangent.shape[-1]
    hidden = down.shape[0]
    heads = width // HEAD_DIM
    upstream_b = jnp.where(scalars[1] == 0, received[...], cotangent[0])
    kept_dy[0] = upstream_b
    d_geglu = dot_nt(upstream_b, down[...])
    gate = kept_up[0, :, :hidden]
    below = normal_below(gate)
    slope = below + gate * jnp.exp(-0.5 * gate * gate) * (2.0 * math.pi) ** -0.5
    kept_dup[0, :, :hidden] = (d_geglu * kept_up[0, :, hidden:] * slope).astype(jnp.bfloat16)
    kept_dup[0, :, hidden:] = (d_geglu * (gate * below)).astype(jnp.bfloat16)
    d_ln_second = dot_nt(kept_dup[0], wide[:, 4 * width : 4 * width + 2 * hidden])
    normed, inverse = normalize(kept_mid[0])
    gain_grads[0, 1:2, :] = jnp.sum(d_ln_second * normed, axis=0, keepdims=True)
    d_middle = upstream_b.astype(jnp.float32) + norm_backward(
        d_ln_second, gains[1:2, :], normed, inverse
    )
    d_middle_b = d_middle.astype(jnp.bfloat16)
    kept_dmid[0] = d_middle_b
    d_attended = dot_nt(d_middle_b, wide[:, 3 * width : 4 * width]).astype(jnp.bfloat16)
    d_queries, d_keys, d_values = [], [], []
    for head in range(heads):
        at = head * HEAD_DIM
        queries = kept_qkv[0, :, at : at + HEAD_DIM]
        keys_rot = kept_qkv[0, :, width + at : width + at + HEAD_DIM]
        values_b = kept_qkv[0, :, 2 * width + at : 2 * width + at + HEAD_DIM]
        d_out = d_attended[:, at : at + HEAD_DIM]
        probs = kept_probs[0, head]
        d_values.append(dot_tn(probs.astype(jnp.bfloat16), d_out))
        d_probs = dot_nt(d_out, values_b)
        row_delta = jnp.sum(probs * d_probs, axis=-1, keepdims=True)
        d_scores = (probs * (d_probs - row_delta)).astype(jnp.bfloat16)
        d_queries.append(dot_nn(d_scores, keys_rot))
        d_keys.append(dot_tn(d_scores, queries))
    cosines = widen(cosine[0], width)
    sines = widen(sine_part[0], width)
    for part, pieces in enumerate((d_queries, d_keys)):
        piece = jnp.concatenate(pieces, axis=1) * (1.0 / HEAD_DIM**0.5)
        kept_dqkv[0, :, part * width : (part + 1) * width] = (
            piece * cosines - swap_halves(piece) * sines
        ).astype(jnp.bfloat16)
    kept_dqkv[0, :, 2 * width :] = jnp.concatenate(d_values, axis=1).astype(jnp.bfloat16)
    d_ln_first = dot_nt(kept_dqkv[0], wide[:, : 3 * width])
    normed, inverse = normalize(kept_x[0].astype(jnp.float32))
    gain_grads[0, 0:1, :] = jnp.sum(d_ln_first * normed, axis=0, keepdims=True)
    outcome = (
        d_middle + norm_backward(d_ln_first, gains[0:1, :], normed, inverse)
    ).astype(jnp.bfloat16)
    result[...] = outcome
    input_grad[0] = outcome


def stage(kernel, name, scalars, blocked, whole, slot_shapes, result_shape, carried):
    def blocked_spec(shape):
        rank = len(shape)
        return pl.BlockSpec(
            (1,) + tuple(shape[1:]), lambda step, picked: (picked[0],) + (0,) * (rank - 1)
        )

    def whole_spec(shape):
        rank = len(shape)
        return pl.BlockSpec(
            tuple(shape), lambda step, picked: (0,) * rank, pipeline_mode=pl.Buffered(1)
        )

    operands, specs = [], []
    for kind, operand in zip(blocked, whole):
        operands.append(operand)
        specs.append(
            blocked_spec(operand.shape) if kind else pl.BlockSpec(memory_space=pltpu.VMEM)
        )
    aliases = {}
    if carried is not None:
        for offset, operand in enumerate(carried):
            aliases[1 + len(operands)] = 1 + offset
            operands.append(operand)
            specs.append(pl.BlockSpec(memory_space=pl.ANY))
    outcome = pl.pallas_call(
        kernel,
        grid_spec=pltpu.PrefetchScalarGridSpec(
            num_scalar_prefetch=1,
            grid=(1,),
            in_specs=specs,
            out_specs=[whole_spec(result_shape.shape)]
            + [blocked_spec(shape.shape) for shape in slot_shapes],
        ),
        out_shape=[result_shape] + list(slot_shapes),
        input_output_aliases=aliases,
        compiler_params=pltpu.CompilerParams(vmem_limit_bytes=28 * 2**20),
        name=name,
    )(scalars, *operands)
    return outcome[0], outcome[1:]


def device_at(ring_place, core, chips):
    half = ring_place // (chips // 2)
    chip = (1 - half) * 2 * ring_place + half * (2 * (chips - 1 - ring_place) + 1)
    return chip * 2 + core


def own_place(chips):
    index = lax.axis_index("dp")
    chip = index // 2
    column = chip % 2
    depth = chip // 2
    return ((1 - column) * depth + column * (chips - 1 - depth), index % 2)


def meet(right, left, sibling):
    barrier = pltpu.get_barrier_semaphore()
    for partner in (right, left, sibling):
        pl.semaphore_signal(
            barrier, inc=1, device_id={"dp": partner}, device_id_type=pl.DeviceIdType.MESH
        )
    pl.semaphore_wait(barrier, 3)


def remote(source, target, send_sem, recv_sem, partner):
    return pltpu.make_async_remote_copy(
        src_ref=source,
        dst_ref=target,
        send_sem=send_sem,
        recv_sem=recv_sem,
        device_id={"dp": partner},
        device_id_type=pl.DeviceIdType.MESH,
    )


def ring_pieces(columns):
    tiles = columns // 128
    half = tiles // 2
    pieces = []
    for way, (first, last) in enumerate(((0, half), (half, tiles))):
        middle = first + (last - first + 1) // 2
        pieces.append((way, pl.ds(first * 128, (middle - first) * 128)))
        pieces.append((way, pl.ds(middle * 128, (last - middle) * 128)))
    return [pieces[0], pieces[2], pieces[1], pieces[3]]


def gather_kernel(chips, shard, full, ring_send, ring_recv, pair_send, pair_recv, own_send, own_recv, local_sem):
    place, core = own_place(chips)
    pieces = ring_pieces(shard.shape[1])
    right = device_at((place + 1) % chips, core, chips)
    left = device_at((place + chips - 1) % chips, core, chips)
    index = device_at(place, core, chips)
    sibling = device_at(place, 1 - core, chips)
    meet(right, left, sibling)
    waiting = []
    ring_copies = []
    for step in range(chips):
        started = []
        for slot, (way, columns) in enumerate(pieces):
            shift = step if way == 1 else chips - step
            block = device_at((place + shift) % chips, core, chips)
            source = shard.at[:, columns] if step == 0 else full.at[block, :, columns]
            target = full.at[block, :, columns]
            if step > 0:
                ring_copies[step - 1][slot].wait_recv()
            if step < chips - 1:
                copy = remote(
                    source,
                    target,
                    ring_send.at[slot, step],
                    ring_recv.at[slot, step],
                    left if way == 1 else right,
                )
                copy.start()
                started.append(copy)
            if step > 0:
                pair = remote(
                    source,
                    target,
                    pair_send.at[slot, step - 1],
                    pair_recv.at[slot, step - 1],
                    sibling,
                )
                pair.start()
                waiting.append(pair)
        if step == 0:
            pair = remote(shard, full.at[index], own_send, own_recv, sibling)
            pair.start()
            waiting.append(pair)
            keep = pltpu.make_async_copy(shard, full.at[index], local_sem)
            keep.start()
        ring_copies.append(started)
    for started in ring_copies:
        for copy in started:
            copy.wait_send()
    for pair in waiting:
        pair.wait()
    keep.wait()


def gather_all(shard):
    count = lax.axis_size("dp")
    chips = count // 2
    dma = pltpu.SemaphoreType.DMA
    return pl.pallas_call(
        functools.partial(gather_kernel, chips),
        out_shape=jax.ShapeDtypeStruct((count,) + shard.shape, shard.dtype),
        in_specs=[pl.BlockSpec(memory_space=pl.ANY)],
        out_specs=pl.BlockSpec(memory_space=pl.ANY),
        scratch_shapes=[dma((4, chips - 1))] * 4 + [dma(())] * 3,
        compiler_params=pltpu.CompilerParams(collective_id=0, has_side_effects=True),
        name="gather_weights",
    )(shard)


def scatter_kernel(chips, parts, total, own, paired, staged, landed, local_sem, pair_send, pair_recv, ring_send, ring_recv):
    place, core = own_place(chips)
    pieces = ring_pieces(total.shape[1])
    right = device_at((place + 1) % chips, core, chips)
    left = device_at((place + chips - 1) % chips, core, chips)
    sibling = device_at(place, 1 - core, chips)
    meet(right, left, sibling)
    pairs = []
    keeps = []
    for hop in range(chips):
        pairs.append([])
        keeps.append([])
        for slot, (way, columns) in enumerate(pieces):
            shift = (1 + hop) if way == 1 else (2 * chips - 1 - hop)
            owner = (place + shift) % chips
            pair = remote(
                parts.at[device_at(owner, 1 - core, chips), :, columns],
                paired.at[hop, :, columns],
                pair_send.at[slot, hop],
                pair_recv.at[slot, hop],
                sibling,
            )
            pair.start()
            pairs[hop].append(pair)
            keep = pltpu.make_async_copy(
                parts.at[device_at(owner, core, chips), :, columns],
                own.at[hop, :, columns],
                local_sem.at[slot, hop],
            )
            keep.start()
            keeps[hop].append(keep)
    copies = []
    for hop in range(chips):
        started = []
        for slot, (way, columns) in enumerate(pieces):
            keeps[hop][slot].wait()
            pairs[hop][slot].wait_recv()
            value = own[hop, :, columns].astype(jnp.float32) + paired[hop, :, columns].astype(
                jnp.float32
            )
            if hop > 0:
                copies[hop - 1][slot].wait_recv()
                value = value + landed[hop - 1, :, columns].astype(jnp.float32)
            if hop < chips - 1:
                staged[hop, :, columns] = value.astype(staged.dtype)
                copy = remote(
                    staged.at[hop, :, columns],
                    landed.at[hop, :, columns],
                    ring_send.at[slot, hop],
                    ring_recv.at[slot, hop],
                    left if way == 1 else right,
                )
                copy.start()
                started.append(copy)
            else:
                total[:, columns] = value
        copies.append(started)
    for started in copies:
        for copy in started:
            copy.wait_send()
    for hop in range(chips):
        for pair in pairs[hop]:
            pair.wait_send()


def scatter_sum(parts):
    count, rows, columns = parts.shape
    chips = count // 2
    dma = pltpu.SemaphoreType.DMA
    return pl.pallas_call(
        functools.partial(scatter_kernel, chips),
        out_shape=jax.ShapeDtypeStruct((rows, columns), jnp.float32),
        in_specs=[pl.BlockSpec(memory_space=pl.ANY)],
        out_specs=pl.BlockSpec(memory_space=pltpu.VMEM),
        scratch_shapes=[
            pltpu.VMEM((chips, rows, columns), parts.dtype),
            pltpu.VMEM((chips, rows, columns), parts.dtype),
            pltpu.VMEM((chips - 1, rows, columns), parts.dtype),
            pltpu.VMEM((chips - 1, rows, columns), parts.dtype),
        ]
        + [dma((4, chips))] * 3
        + [dma((4, chips - 1))] * 2,
        compiler_params=pltpu.CompilerParams(collective_id=1, has_side_effects=True),
        name="scatter_grads",
    )(parts)


def pack_rows(qkv_part, out_part, in_part, down_part, gain_rows):
    rows = qkv_part.shape[-2]
    spare = 2 * rows - down_part.shape[-2]
    tail = jnp.concatenate(
        [
            down_part[..., rows:, :],
            jnp.pad(
                gain_rows,
                [(0, 0)] * (gain_rows.ndim - 2)
                + [(0, spare - 2), (0, down_part.shape[-1] - gain_rows.shape[-1])],
            ),
        ],
        axis=-2,
    )
    return jnp.concatenate([qkv_part, out_part, in_part, down_part[..., :rows, :], tail], axis=-1)


def unpack_rows(packed, model_width, hidden, hidden_share):
    rows = packed.shape[-2]
    rest = hidden_share - rows
    first = 3 * model_width
    second = first + model_width
    third = second + 2 * hidden
    fourth = third + model_width
    down_part = jnp.concatenate(
        [packed[..., third:fourth], packed[..., :rest, fourth:]], axis=-2
    )
    gain_rows = packed[..., rest : rest + 2, fourth : fourth + rows]
    return (
        packed[..., :first],
        packed[..., first:second],
        packed[..., second:third],
        down_part,
        gain_rows,
    )


def body(tokens, cotangent, lengths, w_qkv, w_out, w_in, w_down, gain_attn, gain_mlp):
    section_index = lax.axis_index("section")
    first_section = section_index == 0
    micro_count = lengths.shape[0]
    row_count = tokens.shape[0] // micro_count
    model_width = tokens.shape[1]
    device_count = lax.axis_size("dp")
    feature_share = w_qkv.shape[1]
    hidden_share = w_down.shape[1]
    hidden = hidden_share * device_count
    token_blocks = tokens.reshape(micro_count, row_count, model_width)
    cotangent_blocks = cotangent.reshape(micro_count, row_count, model_width)
    rope_base = jnp.where(first_section, 10000.0, 160000.0).astype(jnp.float32)
    window_reach = jnp.where(first_section, WINDOW, row_count).astype(jnp.int32)
    packed = pack_rows(
        w_qkv[0], w_out[0], w_in[0], w_down[0], jnp.concatenate([gain_attn, gain_mlp], axis=0)
    )
    allowed, positions = jax.vmap(lambda row: pack_layout(row, row_count, window_reach))(lengths)
    allowed = allowed.astype(jnp.float32)
    cosine, sine_part = jax.vmap(lambda places: rotation(places, rope_base))(positions)
    cosine, sine_part = cosine[:, :, 0], sine_part[:, :, 0]
    cosine = jnp.concatenate([cosine] * 4, axis=-1)
    sine_part = jnp.concatenate([-sine_part, sine_part] * 2, axis=-1)
    packed, allowed, cosine, sine_part = lax.optimization_barrier(
        (packed, allowed, cosine, sine_part)
    )
    gathered = gather_all(packed)
    wide = gathered.reshape(-1, gathered.shape[-1])
    down_part, gain_rows = unpack_rows(gathered, model_width, hidden, hidden_share)[3:]
    down = down_part.reshape(hidden, model_width)
    gains = jnp.swapaxes(gain_rows, 0, 1).reshape(2, model_width).astype(jnp.float32)

    def slots(columns, kind=jnp.bfloat16):
        return jax.ShapeDtypeStruct((micro_count, row_count, columns), kind)

    heads = model_width // HEAD_DIM
    block_shape = jax.ShapeDtypeStruct((row_count, model_width), jnp.bfloat16)
    forward_shapes = [
        slots(model_width),
        slots(model_width),
        slots(model_width),
        slots(3 * model_width),
        jax.ShapeDtypeStruct((micro_count, heads, row_count, row_count), jnp.float32),
        slots(model_width),
        slots(model_width, jnp.float32),
        slots(model_width),
        slots(2 * hidden, jnp.float32),
        slots(hidden),
    ]
    received = token_blocks[0]
    kept = None
    for tick_index in range(micro_count + 1):
        slot = jnp.clip(tick_index - section_index, 0, micro_count - 1)
        scalars = jnp.stack([slot, section_index]).astype(jnp.int32)
        result, kept = stage(
            forward_kernel,
            "forward_tick",
            scalars,
            (True, False, True, True, True, False, False, False),
            (token_blocks, received, allowed, cosine, sine_part, wide, down, gains),
            forward_shapes,
            block_shape,
            kept,
        )
        if tick_index < micro_count:
            received = from_behind(result, "section", 1)
    layer_out, inputs_b, ln_first, qkv, probs, attended, middle, ln_second, upward, geglu = kept

    backward_shapes = [
        slots(model_width),
        slots(model_width),
        slots(2 * hidden),
        slots(model_width),
        slots(3 * model_width),
        jax.ShapeDtypeStruct((micro_count, 2, model_width), jnp.float32),
    ]
    received = cotangent_blocks[0]
    kept = None
    for tick_index in range(micro_count + 1):
        slot = jnp.clip(tick_index + section_index - 1, 0, micro_count - 1)
        scalars = jnp.stack([slot, section_index]).astype(jnp.int32)
        result, kept = stage(
            backward_kernel,
            "backward_tick",
            scalars,
            (True, False, True, True, False, False, False, True, True, True, True, True),
            (
                cotangent_blocks, received, cosine, sine_part, wide, down, gains,
                inputs_b, qkv, probs, middle, upward,
            ),
            backward_shapes,
            block_shape,
            kept,
        )
        if tick_index < micro_count:
            received = from_behind(result, "section", -1)
    input_grad, d_out, d_up, d_mid, d_qkv, gain_grads = kept

    def rows_of(slotted):
        return slotted.reshape(micro_count * row_count, slotted.shape[-1])

    def weight_grad(left_side, right_side, share):
        product = contract("rc,rf->cf", rows_of(left_side), rows_of(right_side)).astype(
            jnp.bfloat16
        )
        return product.reshape(device_count, share, product.shape[-1])

    gain_rows = jnp.swapaxes(
        jnp.sum(gain_grads, axis=0).reshape(2, device_count, feature_share), 0, 1
    ).astype(jnp.bfloat16)
    parts = pack_rows(
        weight_grad(ln_first, d_qkv, feature_share),
        weight_grad(attended, d_mid, feature_share),
        weight_grad(ln_second, d_up, feature_share),
        weight_grad(geglu, d_out, hidden_share),
        gain_rows,
    )
    qkv_grad, out_grad, in_grad, down_grad, gain_sums = unpack_rows(
        scatter_sum(parts), model_width, hidden, hidden_share
    )
    return (
        layer_out.reshape(1, micro_count * row_count, model_width),
        input_grad.reshape(1, micro_count * row_count, model_width),
        qkv_grad[None],
        out_grad[None],
        in_grad[None],
        down_grad[None],
        gain_sums[0:1],
        gain_sums[1:2],
    )


def solution(mesh):
    return jax.shard_map(
        body,
        mesh=mesh,
        in_specs=(
            P("dp", None),
            P("dp", None),
            P("dp", None),
            P("section", "dp", None),
            P("section", "dp", None),
            P("section", "dp", None),
            P("section", "dp", None),
            P("section", "dp"),
            P("section", "dp"),
        ),
        out_specs=(
            P("section", "dp", None),
            P("section", "dp", None),
            P("section", "dp", None),
            P("section", "dp", None),
            P("section", "dp", None),
            P("section", "dp", None),
            P("section", "dp"),
            P("section", "dp"),
        ),
        check_vma=False,
    )
```

```python
import functools
import math

import jax
import jax.numpy as jnp
from jax import lax
from jax.experimental import pallas as pl
from jax.experimental.pallas import tpu as pltpu
from jax.sharding import PartitionSpec as P

HEAD_DIM = 64
WINDOW = 64


norm_epsilon = 1e-05


def from_behind(value, axis, steps):
    count = lax.axis_size(axis)
    leading, last = (max(0, -steps), min(count, count - steps))
    return lax.ppermute(value, axis, [(source, source + steps) for source in range(leading, last)])


def contract(formula, left_side, right_side):
    return jnp.einsum(formula, left_side, right_side, preferred_element_type=jnp.float32)


def pack_layout(lengths_row, row_count, window_reach):
    row_ids = jnp.arange(row_count, dtype=jnp.int32)
    doc_ends = jnp.cumsum(lengths_row)
    passed = row_ids[:, None] >= doc_ends[None, :]
    doc_ids = jnp.sum(passed.astype(jnp.int32), axis=1)
    starts = jnp.max(jnp.where(passed, doc_ends[None, :], 0), axis=1)
    positions = row_ids - starts
    allowed = (doc_ids[:, None] == doc_ids[None, :]) & (
        jnp.abs(row_ids[:, None] - row_ids[None, :]) <= window_reach
    )
    return (allowed, positions)


def rotation(positions, rope_base):
    half_dim = HEAD_DIM // 2
    frequency = jnp.exp(
        -jnp.log(rope_base) * (2.0 * jnp.arange(half_dim, dtype=jnp.float32) / HEAD_DIM)
    )
    angles = positions.astype(jnp.float32)[:, None] * frequency[None, :]
    return (jnp.cos(angles)[:, None, :], jnp.sin(angles)[:, None, :])


def normalize(values):
    centered = values - jnp.mean(values, axis=-1, keepdims=True)
    inverse = lax.rsqrt(jnp.mean(centered * centered, axis=-1, keepdims=True) + norm_epsilon)
    return (centered * inverse, inverse)


def norm_backward(upstream, gain_row, normed, inverse):
    scaled = upstream * gain_row
    return inverse * (
        scaled
        - jnp.mean(scaled, axis=-1, keepdims=True)
        - normed * jnp.mean(scaled * normed, axis=-1, keepdims=True)
    )


def swap_halves(values):
    half = HEAD_DIM // 2
    width = values.shape[1]
    lanes = lax.broadcasted_iota(jnp.int32, values.shape, 1)
    return jnp.where(
        lanes % HEAD_DIM < half,
        pltpu.roll(values, width - half, 1),
        pltpu.roll(values, half, 1),
    )


def widen(table, width):
    return jnp.concatenate([table] * (width // table.shape[1]), axis=1)


def dot_nn(left_side, right_side):
    return lax.dot_general(
        left_side, right_side, (((1,), (0,)), ((), ())), preferred_element_type=jnp.float32
    )


def dot_nt(left_side, right_side):
    return lax.dot_general(
        left_side, right_side, (((1,), (1,)), ((), ())), preferred_element_type=jnp.float32
    )


def dot_tn(left_side, right_side):
    return lax.dot_general(
        left_side, right_side, (((0,), (0,)), ((), ())), preferred_element_type=jnp.float32
    )


def normal_below(values):
    return 0.5 * (1.0 + lax.erf(values * (0.5**0.5)))


KEPT = 10


def forward_kernel(scalars, tokens, received, bias, cosine, sine_part, wide, down, gains, *refs):
    result, layer_out, kept_x, kept_ln, kept_qkv, kept_probs, kept_attn, kept_mid, kept_ln2, kept_up, kept_geglu = refs[-KEPT - 1 :]
    width = tokens.shape[-1]
    hidden = down.shape[0]
    heads = width // HEAD_DIM
    inputs_b = jnp.where(scalars[1] == 0, tokens[0], received[...])
    kept_x[0] = inputs_b
    residual = inputs_b.astype(jnp.float32)
    normed, _ = normalize(residual)
    ln_first = (normed * gains[0:1, :]).astype(jnp.bfloat16)
    kept_ln[0] = ln_first
    projected = dot_nn(ln_first, wide[:, : 3 * width])
    cosines = widen(cosine[0], width)
    sines = widen(sine_part[0], width)
    for part in range(2):
        piece = projected[:, part * width : (part + 1) * width]
        kept_qkv[0, :, part * width : (part + 1) * width] = (
            piece * cosines + swap_halves(piece) * sines
        ).astype(jnp.bfloat16)
    kept_qkv[0, :, 2 * width :] = projected[:, 2 * width :].astype(jnp.bfloat16)
    attended = []
    for head in range(heads):
        at = head * HEAD_DIM
        queries = kept_qkv[0, :, at : at + HEAD_DIM]
        keys_rot = kept_qkv[0, :, width + at : width + at + HEAD_DIM]
        values_b = kept_qkv[0, :, 2 * width + at : 2 * width + at + HEAD_DIM]
        scores = jnp.where(
            bias[0] > 0, dot_nt(queries, keys_rot) * (1.0 / HEAD_DIM**0.5), -1e30
        )
        shifted = scores - jnp.max(scores, axis=-1, keepdims=True)
        powers = jnp.exp(shifted)
        probs = powers / jnp.sum(powers, axis=-1, keepdims=True)
        kept_probs[0, head] = probs
        attended.append(dot_nn(probs.astype(jnp.bfloat16), values_b))
    attended = jnp.concatenate(attended, axis=1).astype(jnp.bfloat16)
    kept_attn[0] = attended
    middle = residual + dot_nn(attended, wide[:, 3 * width : 4 * width])
    kept_mid[0] = middle
    normed, _ = normalize(middle)
    ln_second = (normed * gains[1:2, :]).astype(jnp.bfloat16)
    kept_ln2[0] = ln_second
    upward = dot_nn(ln_second, wide[:, 4 * width : 4 * width + 2 * hidden])
    kept_up[0] = upward
    gate = upward[:, :hidden]
    geglu = (gate * normal_below(gate) * upward[:, hidden:]).astype(jnp.bfloat16)
    kept_geglu[0] = geglu
    outcome = (middle + dot_nn(geglu, down[...])).astype(jnp.bfloat16)
    result[...] = outcome
    layer_out[0] = outcome


def backward_kernel(
    scalars, cotangent, received, cosine, sine_part, wide, down, gains,
    kept_x, kept_qkv, kept_probs, kept_mid, kept_up, *refs
):
    result, input_grad, kept_dy, kept_dup, kept_dmid, kept_dqkv, gain_grads = refs[-7:]
    width = cotangent.shape[-1]
    hidden = down.shape[0]
    heads = width // HEAD_DIM
    upstream_b = jnp.where(scalars[1] == 0, received[...], cotangent[0])
    kept_dy[0] = upstream_b
    d_geglu = dot_nt(upstream_b, down[...])
    gate = kept_up[0, :, :hidden]
    below = normal_below(gate)
    slope = below + gate * jnp.exp(-0.5 * gate * gate) * (2.0 * math.pi) ** -0.5
    kept_dup[0, :, :hidden] = (d_geglu * kept_up[0, :, hidden:] * slope).astype(jnp.bfloat16)
    kept_dup[0, :, hidden:] = (d_geglu * (gate * below)).astype(jnp.bfloat16)
    d_ln_second = dot_nt(kept_dup[0], wide[:, 4 * width : 4 * width + 2 * hidden])
    normed, inverse = normalize(kept_mid[0])
    gain_grads[0, 1:2, :] = jnp.sum(d_ln_second * normed, axis=0, keepdims=True)
    d_middle = upstream_b.astype(jnp.float32) + norm_backward(
        d_ln_second, gains[1:2, :], normed, inverse
    )
    d_middle_b = d_middle.astype(jnp.bfloat16)
    kept_dmid[0] = d_middle_b
    d_attended = dot_nt(d_middle_b, wide[:, 3 * width : 4 * width]).astype(jnp.bfloat16)
    d_queries, d_keys, d_values = [], [], []
    for head in range(heads):
        at = head * HEAD_DIM
        queries = kept_qkv[0, :, at : at + HEAD_DIM]
        keys_rot = kept_qkv[0, :, width + at : width + at + HEAD_DIM]
        values_b = kept_qkv[0, :, 2 * width + at : 2 * width + at + HEAD_DIM]
        d_out = d_attended[:, at : at + HEAD_DIM]
        probs = kept_probs[0, head]
        d_values.append(dot_tn(probs.astype(jnp.bfloat16), d_out))
        d_probs = dot_nt(d_out, values_b)
        row_delta = jnp.sum(probs * d_probs, axis=-1, keepdims=True)
        d_scores = (probs * (d_probs - row_delta)).astype(jnp.bfloat16)
        d_queries.append(dot_nn(d_scores, keys_rot))
        d_keys.append(dot_tn(d_scores, queries))
    cosines = widen(cosine[0], width)
    sines = widen(sine_part[0], width)
    for part, pieces in enumerate((d_queries, d_keys)):
        piece = jnp.concatenate(pieces, axis=1) * (1.0 / HEAD_DIM**0.5)
        kept_dqkv[0, :, part * width : (part + 1) * width] = (
            piece * cosines - swap_halves(piece) * sines
        ).astype(jnp.bfloat16)
    kept_dqkv[0, :, 2 * width :] = jnp.concatenate(d_values, axis=1).astype(jnp.bfloat16)
    d_ln_first = dot_nt(kept_dqkv[0], wide[:, : 3 * width])
    normed, inverse = normalize(kept_x[0].astype(jnp.float32))
    gain_grads[0, 0:1, :] = jnp.sum(d_ln_first * normed, axis=0, keepdims=True)
    outcome = (
        d_middle + norm_backward(d_ln_first, gains[0:1, :], normed, inverse)
    ).astype(jnp.bfloat16)
    result[...] = outcome
    input_grad[0] = outcome


def stage(kernel, name, scalars, blocked, whole, slot_shapes, result_shape, carried):
    def blocked_spec(shape):
        rank = len(shape)
        return pl.BlockSpec(
            (1,) + tuple(shape[1:]), lambda step, picked: (picked[0],) + (0,) * (rank - 1)
        )

    def whole_spec(shape):
        rank = len(shape)
        return pl.BlockSpec(
            tuple(shape), lambda step, picked: (0,) * rank, pipeline_mode=pl.Buffered(1)
        )

    operands, specs = [], []
    for kind, operand in zip(blocked, whole):
        operands.append(operand)
        specs.append(blocked_spec(operand.shape) if kind else whole_spec(operand.shape))
    aliases = {}
    if carried is not None:
        for offset, operand in enumerate(carried):
            aliases[1 + len(operands)] = 1 + offset
            operands.append(operand)
            specs.append(pl.BlockSpec(memory_space=pl.ANY))
    outcome = pl.pallas_call(
        kernel,
        grid_spec=pltpu.PrefetchScalarGridSpec(
            num_scalar_prefetch=1,
            grid=(1,),
            in_specs=specs,
            out_specs=[whole_spec(result_shape.shape)]
            + [blocked_spec(shape.shape) for shape in slot_shapes],
        ),
        out_shape=[result_shape] + list(slot_shapes),
        input_output_aliases=aliases,
        compiler_params=pltpu.CompilerParams(vmem_limit_bytes=60000 * 1024),
        name=name,
    )(scalars, *operands)
    return outcome[0], outcome[1:]


def device_at(ring_place, core, chips):
    half = ring_place // (chips // 2)
    chip = (1 - half) * 2 * ring_place + half * (2 * (chips - 1 - ring_place) + 1)
    return chip * 2 + core


def own_place(chips):
    index = lax.axis_index("dp")
    chip = index // 2
    column = chip % 2
    depth = chip // 2
    return ((1 - column) * depth + column * (chips - 1 - depth), index % 2)


def meet(right, left, sibling):
    barrier = pltpu.get_barrier_semaphore()
    for partner in (right, left, sibling):
        pl.semaphore_signal(
            barrier, inc=1, device_id={"dp": partner}, device_id_type=pl.DeviceIdType.MESH
        )
    pl.semaphore_wait(barrier, 3)


def remote(source, target, send_sem, recv_sem, partner):
    return pltpu.make_async_remote_copy(
        src_ref=source,
        dst_ref=target,
        send_sem=send_sem,
        recv_sem=recv_sem,
        device_id={"dp": partner},
        device_id_type=pl.DeviceIdType.MESH,
    )


def ring_pieces(columns):
    tiles = columns // 128
    half = tiles // 2
    pieces = []
    for way, (first, last) in enumerate(((0, half), (half, tiles))):
        middle = first + (last - first + 1) // 2
        pieces.append((way, pl.ds(first * 128, (middle - first) * 128)))
        pieces.append((way, pl.ds(middle * 128, (last - middle) * 128)))
    return [pieces[0], pieces[2], pieces[1], pieces[3]]


def gather_kernel(chips, shard, full, ring_send, ring_recv, pair_send, pair_recv, own_send, own_recv, local_sem):
    place, core = own_place(chips)
    pieces = ring_pieces(shard.shape[1])
    right = device_at((place + 1) % chips, core, chips)
    left = device_at((place + chips - 1) % chips, core, chips)
    index = device_at(place, core, chips)
    sibling = device_at(place, 1 - core, chips)
    meet(right, left, sibling)
    waiting = []
    ring_copies = []
    for step in range(chips):
        started = []
        for slot, (way, columns) in enumerate(pieces):
            shift = step if way == 1 else chips - step
            block = device_at((place + shift) % chips, core, chips)
            source = shard.at[:, columns] if step == 0 else full.at[block, :, columns]
            target = full.at[block, :, columns]
            if step > 0:
                ring_copies[step - 1][slot].wait_recv()
            if step < chips - 1:
                copy = remote(
                    source,
                    target,
                    ring_send.at[slot, step],
                    ring_recv.at[slot, step],
                    left if way == 1 else right,
                )
                copy.start()
                started.append(copy)
            if step > 0:
                pair = remote(
                    source,
                    target,
                    pair_send.at[slot, step - 1],
                    pair_recv.at[slot, step - 1],
                    sibling,
                )
                pair.start()
                waiting.append(pair)
        if step == 0:
            pair = remote(shard, full.at[index], own_send, own_recv, sibling)
            pair.start()
            waiting.append(pair)
            keep = pltpu.make_async_copy(shard, full.at[index], local_sem)
            keep.start()
        ring_copies.append(started)
    for started in ring_copies:
        for copy in started:
            copy.wait_send()
    for pair in waiting:
        pair.wait()
    keep.wait()


def gather_all(shard):
    count = lax.axis_size("dp")
    chips = count // 2
    dma = pltpu.SemaphoreType.DMA
    return pl.pallas_call(
        functools.partial(gather_kernel, chips),
        out_shape=jax.ShapeDtypeStruct((count,) + shard.shape, shard.dtype),
        in_specs=[pl.BlockSpec(memory_space=pl.ANY)],
        out_specs=pl.BlockSpec(memory_space=pl.ANY),
        scratch_shapes=[dma((4, chips - 1))] * 4 + [dma(())] * 3,
        compiler_params=pltpu.CompilerParams(collective_id=0, has_side_effects=True),
        name="gather_weights",
    )(shard)


def scatter_kernel(chips, parts, total, own, paired, staged, landed, local_sem, pair_send, pair_recv, ring_send, ring_recv):
    place, core = own_place(chips)
    pieces = ring_pieces(total.shape[1])
    rows = total.shape[0]
    group = 16 if rows % 16 == 0 else rows
    right = device_at((place + 1) % chips, core, chips)
    left = device_at((place + chips - 1) % chips, core, chips)
    sibling = device_at(place, 1 - core, chips)
    meet(right, left, sibling)
    pairs = []
    keeps = []
    for hop in range(chips):
        pairs.append([])
        keeps.append([])
        for slot, (way, columns) in enumerate(pieces):
            shift = (1 + hop) if way == 1 else (2 * chips - 1 - hop)
            owner = (place + shift) % chips
            pair = remote(
                parts.at[device_at(owner, 1 - core, chips), :, columns],
                paired.at[hop, :, columns],
                pair_send.at[slot, hop],
                pair_recv.at[slot, hop],
                sibling,
            )
            pair.start()
            pairs[hop].append(pair)
            keep = pltpu.make_async_copy(
                parts.at[device_at(owner, core, chips), :, columns],
                own.at[hop, :, columns],
                local_sem.at[slot, hop],
            )
            keep.start()
            keeps[hop].append(keep)
    copies = []
    for hop in range(chips):
        started = []
        for slot, (way, columns) in enumerate(pieces):
            keeps[hop][slot].wait()
            pairs[hop][slot].wait_recv()
            if hop > 0:
                copies[hop - 1][slot].wait_recv()

            def add_rows(step, carry, hop=hop, columns=columns):
                at = pl.ds(step * group, group)
                value = own[hop, at, columns].astype(jnp.float32) + paired[
                    hop, at, columns
                ].astype(jnp.float32)
                if hop > 0:
                    value = value + landed[hop - 1, at, columns].astype(jnp.float32)
                if hop < chips - 1:
                    staged[hop, at, columns] = value.astype(staged.dtype)
                else:
                    total[at, columns] = value
                return carry

            lax.fori_loop(0, rows // group, add_rows, 0)
            if hop < chips - 1:
                copy = remote(
                    staged.at[hop, :, columns],
                    landed.at[hop, :, columns],
                    ring_send.at[slot, hop],
                    ring_recv.at[slot, hop],
                    left if way == 1 else right,
                )
                copy.start()
                started.append(copy)
        copies.append(started)
    for started in copies:
        for copy in started:
            copy.wait_send()
    for hop in range(chips):
        for pair in pairs[hop]:
            pair.wait_send()


def scatter_sum(parts):
    count, rows, columns = parts.shape
    chips = count // 2
    dma = pltpu.SemaphoreType.DMA
    return pl.pallas_call(
        functools.partial(scatter_kernel, chips),
        out_shape=jax.ShapeDtypeStruct((rows, columns), jnp.float32),
        in_specs=[pl.BlockSpec(memory_space=pl.ANY)],
        out_specs=pl.BlockSpec(memory_space=pltpu.VMEM),
        scratch_shapes=[
            pltpu.VMEM((chips, rows, columns), parts.dtype),
            pltpu.VMEM((chips, rows, columns), parts.dtype),
            pltpu.VMEM((chips - 1, rows, columns), parts.dtype),
            pltpu.VMEM((chips - 1, rows, columns), parts.dtype),
        ]
        + [dma((4, chips))] * 3
        + [dma((4, chips - 1))] * 2,
        compiler_params=pltpu.CompilerParams(collective_id=1, has_side_effects=True),
        name="scatter_grads",
    )(parts)


def pack_rows(qkv_part, out_part, in_part, down_part, gain_rows):
    rows = qkv_part.shape[-2]
    spare = 2 * rows - down_part.shape[-2]
    tail = jnp.concatenate(
        [
            down_part[..., rows:, :],
            jnp.pad(
                gain_rows,
                [(0, 0)] * (gain_rows.ndim - 2)
                + [(0, spare - 2), (0, down_part.shape[-1] - gain_rows.shape[-1])],
            ),
        ],
        axis=-2,
    )
    return jnp.concatenate([qkv_part, out_part, in_part, down_part[..., :rows, :], tail], axis=-1)


def unpack_rows(packed, model_width, hidden, hidden_share):
    rows = packed.shape[-2]
    rest = hidden_share - rows
    first = 3 * model_width
    second = first + model_width
    third = second + 2 * hidden
    fourth = third + model_width
    down_part = jnp.concatenate(
        [packed[..., third:fourth], packed[..., :rest, fourth:]], axis=-2
    )
    gain_rows = packed[..., rest : rest + 2, fourth : fourth + rows]
    return (
        packed[..., :first],
        packed[..., first:second],
        packed[..., second:third],
        down_part,
        gain_rows,
    )


def body(tokens, cotangent, lengths, w_qkv, w_out, w_in, w_down, gain_attn, gain_mlp):
    section_index = lax.axis_index("section")
    first_section = section_index == 0
    micro_count = lengths.shape[0]
    row_count = tokens.shape[0] // micro_count
    model_width = tokens.shape[1]
    device_count = lax.axis_size("dp")
    feature_share = w_qkv.shape[1]
    hidden_share = w_down.shape[1]
    hidden = hidden_share * device_count
    token_blocks = tokens.reshape(micro_count, row_count, model_width)
    cotangent_blocks = cotangent.reshape(micro_count, row_count, model_width)
    rope_base = jnp.where(first_section, 10000.0, 160000.0).astype(jnp.float32)
    window_reach = jnp.where(first_section, WINDOW, row_count).astype(jnp.int32)
    packed = pack_rows(
        w_qkv[0], w_out[0], w_in[0], w_down[0], jnp.concatenate([gain_attn, gain_mlp], axis=0)
    )
    allowed, positions = jax.vmap(lambda row: pack_layout(row, row_count, window_reach))(lengths)
    allowed = allowed.astype(jnp.float32)
    cosine, sine_part = jax.vmap(lambda places: rotation(places, rope_base))(positions)
    cosine, sine_part = cosine[:, :, 0], sine_part[:, :, 0]
    cosine = jnp.concatenate([cosine] * 4, axis=-1)
    sine_part = jnp.concatenate([-sine_part, sine_part] * 2, axis=-1)
    packed, allowed, cosine, sine_part = lax.optimization_barrier(
        (packed, allowed, cosine, sine_part)
    )
    gathered = gather_all(packed)
    wide = gathered.reshape(-1, gathered.shape[-1])
    down_part, gain_rows = unpack_rows(gathered, model_width, hidden, hidden_share)[3:]
    down = down_part.reshape(hidden, model_width)
    gains = jnp.swapaxes(gain_rows, 0, 1).reshape(2, model_width).astype(jnp.float32)

    def slots(columns, kind=jnp.bfloat16):
        return jax.ShapeDtypeStruct((micro_count, row_count, columns), kind)

    heads = model_width // HEAD_DIM
    block_shape = jax.ShapeDtypeStruct((row_count, model_width), jnp.bfloat16)
    forward_shapes = [
        slots(model_width),
        slots(model_width),
        slots(model_width),
        slots(3 * model_width),
        jax.ShapeDtypeStruct((micro_count, heads, row_count, row_count), jnp.float32),
        slots(model_width),
        slots(model_width, jnp.float32),
        slots(model_width),
        slots(2 * hidden, jnp.float32),
        slots(hidden),
    ]
    received = token_blocks[0]
    kept = None
    for tick_index in range(micro_count + 1):
        slot = jnp.clip(tick_index - section_index, 0, micro_count - 1)
        scalars = jnp.stack([slot, section_index]).astype(jnp.int32)
        result, kept = stage(
            forward_kernel,
            "forward_tick",
            scalars,
            (True, False, True, True, True, False, False, False),
            (token_blocks, received, allowed, cosine, sine_part, wide, down, gains),
            forward_shapes,
            block_shape,
            kept,
        )
        if tick_index < micro_count:
            received = from_behind(result, "section", 1)
    layer_out, inputs_b, ln_first, qkv, probs, attended, middle, ln_second, upward, geglu = kept

    backward_shapes = [
        slots(model_width),
        slots(model_width),
        slots(2 * hidden),
        slots(model_width),
        slots(3 * model_width),
        jax.ShapeDtypeStruct((micro_count, 2, model_width), jnp.float32),
    ]
    received = cotangent_blocks[0]
    kept = None
    for tick_index in range(micro_count + 1):
        slot = jnp.clip(tick_index + section_index - 1, 0, micro_count - 1)
        scalars = jnp.stack([slot, section_index]).astype(jnp.int32)
        result, kept = stage(
            backward_kernel,
            "backward_tick",
            scalars,
            (True, False, True, True, False, False, False, True, True, True, True, True),
            (
                cotangent_blocks, received, cosine, sine_part, wide, down, gains,
                inputs_b, qkv, probs, middle, upward,
            ),
            backward_shapes,
            block_shape,
            kept,
        )
        if tick_index < micro_count:
            received = from_behind(result, "section", -1)
    input_grad, d_out, d_up, d_mid, d_qkv, gain_grads = kept

    def rows_of(slotted):
        return slotted.reshape(micro_count * row_count, slotted.shape[-1])

    def weight_grad(left_side, right_side, share):
        product = contract("rc,rf->cf", rows_of(left_side), rows_of(right_side)).astype(
            jnp.bfloat16
        )
        return product.reshape(device_count, share, product.shape[-1])

    gain_rows = jnp.swapaxes(
        jnp.sum(gain_grads, axis=0).reshape(2, device_count, feature_share), 0, 1
    ).astype(jnp.bfloat16)
    parts = pack_rows(
        weight_grad(ln_first, d_qkv, feature_share),
        weight_grad(attended, d_mid, feature_share),
        weight_grad(ln_second, d_up, feature_share),
        weight_grad(geglu, d_out, hidden_share),
        gain_rows,
    )
    qkv_grad, out_grad, in_grad, down_grad, gain_sums = unpack_rows(
        scatter_sum(parts), model_width, hidden, hidden_share
    )
    return (
        layer_out.reshape(1, micro_count * row_count, model_width),
        input_grad.reshape(1, micro_count * row_count, model_width),
        qkv_grad[None],
        out_grad[None],
        in_grad[None],
        down_grad[None],
        gain_sums[0:1],
        gain_sums[1:2],
    )


def solution(mesh):
    return jax.shard_map(
        body,
        mesh=mesh,
        in_specs=(
            P("dp", None),
            P("dp", None),
            P("dp", None),
            P("section", "dp", None),
            P("section", "dp", None),
            P("section", "dp", None),
            P("section", "dp", None),
            P("section", "dp"),
            P("section", "dp"),
        ),
        out_specs=(
            P("section", "dp", None),
            P("section", "dp", None),
            P("section", "dp", None),
            P("section", "dp", None),
            P("section", "dp", None),
            P("section", "dp", None),
            P("section", "dp"),
            P("section", "dp"),
        ),
        check_vma=False,
    )
```
